32 devices in a mesh: pair: 4 (over x, core), blk: 8 (over z, y).
Axes of the slice: x: 2, y: 2, z: 4, core: 2. Of those that a mesh axis runs over, the one named last changes fastest.
Arguments:
- left_feats: bfloat16 [4, 64, 256, 256], P('pair', None, 'blk'), may hold values from -6 to 6
- right_feats: bfloat16 [4, 64, 256, 256], P('pair', None, 'blk'), may hold values from -6 to 6
- offsets: int32 [8], P('blk'), may hold values from 0 to 3, as said below
- hidden: bfloat16 [4, 64, 256, 128], P('pair', None, 'blk'), may hold values from -1 to 1
- context: bfloat16 [4, 3, 64, 256, 128], P('pair', None, None, 'blk'), may hold values from -6 to 6
- gru_weights: bfloat16 [2, 3, 5, 164, 128], replicated, may hold values from -0.21875 to 0.21875
- hidden_grad: float32 [4, 64, 256, 128], P('pair', None, 'blk'), may hold values from -0.06 to 0.06
Outputs:
- new_hidden: bfloat16 [4, 64, 256, 128], P('pair', None, 'blk')
- weight_grads: float32 [2, 3, 5, 164, 128], replicated
- hidden_in_grad: float32 [4, 64, 256, 128], P('pair', None, 'blk')
The draws below stay inside these ranges and needn't reach their ends.
Inputs may be any that keep to these rules, and one draw needn't show every extreme that they name: Stripe s reads the frame-2 blocks s - offsets[s] - 1 and s - offsets[s]; some stripe has offset 4 - 1.
All inputs are finite; a program needn't handle non-finite values.
Results may differ from the reference program's by a relative error of at most 0.0054.
Values may be sent and summed in bfloat16 or wider, within the bound.
A program may use at most 128 MiB of HBM per device.

```python
import functools
import math
import jax
import jax.numpy as jnp
import numpy as np
from jax import lax

C = 256
HD = 128
LEVELS = 4
RADIUS = 4
KS = 5
BAND = 4
ROWS = 64
COLS = 32
CORR = 36
STRIPES = 8
WIDTH = 256
PAIRS = 4


def draw_offsets(key, part):
    first_key, second_key = jax.random.split(jax.random.fold_in(key, 17))
    values = jax.random.randint(first_key, (STRIPES,), 0, BAND, dtype=jnp.int32)
    chosen = jax.random.randint(second_key, (), 0, STRIPES, dtype=jnp.int32)
    return jnp.where(jnp.arange(STRIPES, dtype=jnp.int32) == chosen, BAND - 1, values).astype(jnp.int32)


def level_of(stream_key, dims, pieces, low, high):
    loudness = 1.0
    for position, shards_of in pieces:
        heights = jax.random.uniform(jax.random.fold_in(jax.random.fold_in(stream_key, 6), position), (shards_of,), jnp.float32, low / len(pieces), high / len(pieces))
        loudness = loudness * jnp.repeat(jnp.exp(heights), dims[position] // shards_of).reshape((-1,) + (1,) * (len(dims) - 1 - position))
    return loudness


def normal_values(rng, shape, width, most, cuts=(), kind=jnp.bfloat16):
    factor_of = level_of(rng, shape, cuts, -0.22, 0.18) if cuts else 1.0
    entries = jax.random.normal(rng, shape, jnp.float32) * width * factor_of
    return jnp.minimum(jnp.maximum(entries, -most), most).astype(kind)


def setup_inputs(seed: int = 0) -> dict:
    splits = jax.random.split(jax.random.key(seed), 8)
    return {
        "left_feats": normal_values(splits[0], (PAIRS, ROWS, WIDTH, C), 1.0, 6.0, ((0, 4), (2, 8))),
        "right_feats": normal_values(splits[1], (PAIRS, ROWS, WIDTH, C), 1.0, 6.0, ((0, 4), (2, 8))),
        "offsets": draw_offsets(jax.random.fold_in(splits[7], 71), 0),
        "hidden": jnp.clip(jax.random.uniform(splits[3], (PAIRS, ROWS, WIDTH, HD), jnp.float32, -1.0, 1.0) * level_of(splits[3], (PAIRS, ROWS, WIDTH, HD), ((0, 4), (2, 8)), -0.4, 0.0), -1.0, 1.0).astype(jnp.bfloat16),
        "context": normal_values(splits[4], (PAIRS, 3, ROWS, WIDTH, HD), 1.0, 6.0, ((0, 4), (3, 8))),
        "gru_weights": normal_values(splits[5], (2, 3, KS, HD + CORR, HD), (KS * (HD + CORR)) ** -0.5, 0.21875),
        "hidden_grad": normal_values(splits[6], (PAIRS, ROWS, WIDTH, HD), 0.01, 0.06, ((0, 4), (2, 8)), jnp.float32),
    }


def lookup_table(column_count, level_count, radius_len):
    tap_count = 2 * radius_len + 1
    lookup = np.zeros((column_count, 2 * column_count, level_count * tap_count), np.float32)
    positions = np.arange(column_count)
    for level_id in range(level_count):
        pool_span = 2 ** level_id
        pooled_cols = 2 * column_count // pool_span
        for tap_id in range(tap_count):
            centre = (positions + column_count // 2) // pool_span + tap_id - radius_len
            inside = (centre >= 0) & (centre < pooled_cols)
            for inner_id in range(pool_span):
                lookup[positions[inside], centre[inside] * pool_span + inner_id, level_id * tap_count + tap_id] = 1.0 / pool_span
    return lookup

def tap_stack(padded, extent, axis_dim, kernel_len):
    return jnp.concatenate([lax.slice_in_dim(padded, tap_id, tap_id + extent, axis=axis_dim) for tap_id in range(kernel_len)], axis=-1)

def conv_apply(padded, weight_taps, extent, axis_dim):
    kernel_len, in_chan, out_chan = weight_taps.shape
    stacked = tap_stack(padded, extent, axis_dim, kernel_len)
    flat_taps = stacked.reshape(-1, kernel_len * in_chan)
    result = jnp.dot(flat_taps, weight_taps.reshape(kernel_len * in_chan, out_chan), preferred_element_type=jnp.float32)
    return result.reshape(stacked.shape[:-1] + (out_chan,))

def conv_weight_grad(padded, deltas, axis_dim):
    extent = deltas.shape[axis_dim]
    kernel_len = padded.shape[axis_dim] - extent + 1
    stacked = tap_stack(padded, extent, axis_dim, kernel_len)
    flat_taps = stacked.reshape(-1, stacked.shape[-1])
    flat_deltas = deltas.reshape(-1, deltas.shape[-1])
    result = lax.dot_general(flat_taps, flat_deltas, (((0,), (0,)), ((), ())), preferred_element_type=jnp.float32)
    return result.reshape(kernel_len, padded.shape[-1], deltas.shape[-1])

def conv_input_grad(deltas, weight_taps, axis_dim):
    kernel_len, in_chan, out_chan = weight_taps.shape
    backward_taps = lax.dot_general(deltas.reshape(-1, out_chan), weight_taps.reshape(kernel_len * in_chan, out_chan), (((1,), (1,)), ((), ())), preferred_element_type=jnp.float32)
    backward_taps = backward_taps.reshape(deltas.shape[:-1] + (kernel_len * in_chan,))
    summed = None
    for tap_id in range(kernel_len):
        tap_part = backward_taps[..., tap_id * in_chan:(tap_id + 1) * in_chan]
        widths = [(0, 0)] * deltas.ndim
        widths[axis_dim] = (tap_id, kernel_len - 1 - tap_id)
        shifted = jnp.pad(tap_part, widths)
        summed = shifted if summed is None else summed + shifted
    return summed

def pad_along(values, axis_dim):
    widths = [(0, 0)] * values.ndim
    widths[axis_dim] = (2, 2)
    return jnp.pad(values, widths)

def crop_along(values, axis_dim):
    extent = values.shape[axis_dim] - 4
    return lax.slice_in_dim(values, 2, extent + 2, axis=axis_dim)

def section_forward(padded, context_parts, weights, axis_dim, extend):
    extent = padded.shape[axis_dim] - 4
    hidden_width = weights.shape[-1]
    own_inputs = lax.slice_in_dim(padded, 2, extent + 2, axis=axis_dim)
    hidden_own = own_inputs[..., :hidden_width].astype(jnp.float32)
    feat_padded = padded[..., hidden_width:]
    update_gate = jax.nn.sigmoid(conv_apply(padded, weights[0], extent, axis_dim) + context_parts[0].astype(jnp.float32))
    reset_gate = jax.nn.sigmoid(conv_apply(padded, weights[1], extent, axis_dim) + context_parts[1].astype(jnp.float32))
    reset_hidden = (reset_gate * hidden_own).astype(jnp.bfloat16)
    gated_padded = jnp.concatenate([extend(reset_hidden), feat_padded], axis=-1)
    candidate = jnp.tanh(conv_apply(gated_padded, weights[2], extent, axis_dim) + context_parts[2].astype(jnp.float32))
    blended = (1.0 - update_gate) * hidden_own + update_gate * candidate
    return (blended, (update_gate, reset_gate, candidate, hidden_own, padded, gated_padded))

def section_backward(cotangent, stored, weights, axis_dim, fold_rims, want_hidden):
    update_gate, reset_gate, candidate, hidden_own, padded, gated_padded = stored
    hidden_width = weights.shape[-1]
    delta_cand = (cotangent * update_gate * (1.0 - candidate * candidate)).astype(jnp.bfloat16)
    grad_cand = conv_weight_grad(gated_padded, delta_cand, axis_dim)
    back_gated = fold_rims(conv_input_grad(delta_cand, weights[2][:, :hidden_width], axis_dim))
    delta_update = (cotangent * (candidate - hidden_own) * update_gate * (1.0 - update_gate)).astype(jnp.bfloat16)
    delta_reset = (back_gated * hidden_own * reset_gate * (1.0 - reset_gate)).astype(jnp.bfloat16)
    grad_update = conv_weight_grad(padded, delta_update, axis_dim)
    grad_reset = conv_weight_grad(padded, delta_reset, axis_dim)
    grad_stack = jnp.stack([grad_update, grad_reset, grad_cand])
    if want_hidden:
        back_inputs = conv_input_grad(delta_update, weights[0][:, :hidden_width], axis_dim) + conv_input_grad(delta_reset, weights[1][:, :hidden_width], axis_dim)
        hidden_back = cotangent * (1.0 - update_gate) + back_gated * reset_gate + fold_rims(back_inputs)
        return (grad_stack, hidden_back)
    return (grad_stack, None)

def reference(left_feats, right_feats, offsets, hidden, context, gru_weights, hidden_grad):
    lookup = jnp.asarray(lookup_table(COLS, LEVELS, RADIUS))
    inv_scale = 1.0 / math.sqrt(C)
    block_index = jnp.arange(STRIPES, dtype=jnp.int32) - offsets.astype(jnp.int32) + BAND
    outputs = []
    input_grads = []
    summed = jnp.zeros(gru_weights.shape, jnp.float32)
    for pair_index in range(PAIRS):
        left_rows = left_feats[pair_index].reshape(ROWS, STRIPES, COLS, C)
        blocks = right_feats[pair_index].reshape(ROWS, STRIPES, COLS, C)
        padded_blocks = jnp.concatenate([jnp.zeros((ROWS, BAND, COLS, C), jnp.bfloat16), blocks], axis=1)
        window = jnp.concatenate([jnp.take(padded_blocks, block_index - 1, axis=1), jnp.take(padded_blocks, block_index, axis=1)], axis=2)
        scores = jnp.einsum('hnxc,hnjc->hnxj', left_rows.astype(jnp.float32), window.astype(jnp.float32)) * inv_scale
        features = jnp.einsum('hnxj,xjf->hnxf', scores, lookup, precision=lax.Precision.HIGHEST)
        features = features.reshape(ROWS, WIDTH, CORR).astype(jnp.bfloat16)
        context_parts = context[pair_index]
        first_inputs = jnp.concatenate([hidden[pair_index], features], axis=-1)
        first_new, first_stored = section_forward(pad_along(first_inputs, 1), context_parts, gru_weights[0], 1, functools.partial(pad_along, axis_dim=1))
        first_hidden = first_new.astype(jnp.bfloat16)
        second_inputs = jnp.concatenate([first_hidden, features], axis=-1)
        second_new, second_stored = section_forward(pad_along(second_inputs, 0), context_parts, gru_weights[1], 0, functools.partial(pad_along, axis_dim=0))
        outputs.append(second_new.astype(jnp.bfloat16))
        second_grads, first_back = section_backward(hidden_grad[pair_index], second_stored, gru_weights[1], 0, functools.partial(crop_along, axis_dim=0), True)
        first_grads, hidden_back = section_backward(first_back, first_stored, gru_weights[0], 1, functools.partial(crop_along, axis_dim=1), True)
        input_grads.append(hidden_back)
        summed = summed + jnp.stack([first_grads, second_grads])
    return (jnp.stack(outputs), summed, jnp.stack(input_grads))
```

```python
import functools
import math

import jax
import jax.numpy as jnp
import numpy as np
from jax import lax
from jax.experimental import pallas as pl
from jax.experimental.pallas import tpu as pltpu
from jax.sharding import PartitionSpec as P

LEVELS = 4
RADIUS = 4


def lookup_table(column_count, level_count, radius_len):
    tap_count = 2 * radius_len + 1
    lookup = np.zeros((column_count, 2 * column_count, level_count * tap_count), np.float32)
    positions = np.arange(column_count)
    for level_id in range(level_count):
        pool_span = 2**level_id
        pooled_cols = 2 * column_count // pool_span
        for tap_id in range(tap_count):
            centre = (positions + column_count // 2) // pool_span + tap_id - radius_len
            inside = (centre >= 0) & (centre < pooled_cols)
            for inner_id in range(pool_span):
                lookup[
                    positions[inside],
                    centre[inside] * pool_span + inner_id,
                    level_id * tap_count + tap_id,
                ] = (
                    1.0 / pool_span
                )
    return lookup


def packed_table(lookup, lanes):
    width, _, feats = lookup.shape
    groups = lanes // width
    span = width // groups
    table = np.zeros((span, 2, groups, width, groups, lanes), np.float32)
    for group in range(groups):
        columns = lookup[group * span : (group + 1) * span].reshape(span, 2, width, feats)
        table[:, :, group, :, group, :feats] = columns
    return table.reshape(span, 2 * lanes, groups * lanes)


MESH = pl.DeviceIdType.MESH
BAND_CHUNKS = 8


def sum_steps(pairs, blks):
    steps = []
    for axis, size, most in (("pair", pairs, 2), ("blk", blks, 8)):
        stride = 1
        while stride < size:
            members = min(most, size // stride)
            steps.append((axis, stride, members))
            stride *= members
    return steps


def sum_rows_count(used, devices):
    step = devices * 16
    return -(-used // step) * step


NT = (((1,), (1,)), ((), ()))


def flat(values):
    return values.reshape(-1, values.shape[-1])


def core_kernel(
    count,
    piece,
    steps,
    offset_ref,
    block_in,
    left_in,
    table_in,
    hidden_in,
    context_in,
    weights_in,
    grad_in,
    new_ref,
    hidden_back_ref,
    sum_ref,
    right_ref,
    prior_ref,
    left_ref,
    first_ref,
    second_ref,
    scores,
    notes,
    table_ref,
    hidden_ref,
    context_ref,
    narrow_ref,
    grad_ref,
    weights_ref,
    g_ref,
    sbuf,
    rbuf,
    x0,
    x1,
    rx0,
    rx1,
    dq0,
    dq1,
    dzr0,
    dzr1,
    ctx0,
    z0,
    r0,
    q0,
    z1,
    r1,
    g0,
    acc,
    send_sem,
    recv_sem,
    block_send,
    block_recv,
    score_send,
    score_recv,
    note_send,
    note_recv,
    sum_send,
    sum_recv,
    local_sem,
):
    height, width, hd = hidden_ref.shape
    taps = weights_ref.shape[2]
    me = lax.axis_index("blk")
    has_left = me >= 1
    has_right = me + 1 < count
    bf16, f32 = jnp.bfloat16, jnp.float32
    part = 16

    for ref in (x0, x1, rx0, rx1, dq0, dq1, dzr0, dzr1):
        edge = jnp.zeros((2,) + ref.shape[1:], bf16)
        ref[pl.ds(0, 2)] = edge
        ref[pl.ds(ref.shape[0] - 2, 2)] = edge

    @pl.when(me < 2)
    def _():
        prior_ref[...] = jnp.zeros(prior_ref.shape, bf16)
        scores[4] = jnp.zeros(scores.shape[1:], bf16)

    @pl.when(me < 1)
    def _():
        scores[3] = jnp.zeros(scores.shape[1:], bf16)

    offset = offset_ref[0]
    notes[1] = jnp.full(notes.shape[1:], offset, jnp.int32).astype(f32)

    barrier = pltpu.get_barrier_semaphore()
    places = {"pair": lax.axis_index("pair"), "blk": me}
    ranks = []
    partners = []
    for axis, stride, members in steps:
        place = places[axis]
        ranks.append(lax.rem(place // stride, members))
        row = [None]
        for d in range(1, members):
            shift = 0
            mask = 1
            while mask < members:
                if d & mask:
                    bit = lax.rem(place // (stride * mask), 2)
                    shift = shift + stride * mask * (1 - 2 * bit)
                mask *= 2
            row.append((place + shift, axis))
            pl.semaphore_signal(barrier, inc=1, device_id={axis: place + shift}, device_id_type=MESH)
        partners.append(row)
    has_next = me + 2 < count
    has_prev = me >= 2
    expected = sum(members - 1 for _, _, members in steps)
    for present, shift in ((has_left, -1), (has_right, 1), (has_prev, -2), (has_next, 2)):

        @pl.when(present)
        def _(shift=shift):
            pl.semaphore_signal(barrier, inc=1, device_id={"blk": me + shift}, device_id_type=MESH)

        expected = expected + present.astype(jnp.int32)
    pl.semaphore_wait(barrier, expected)

    odd = lax.rem(me, 2)
    mate = me + 1 - 2 * odd
    band_rows = height // BAND_CHUNKS

    AHEAD, BEHIND, BESIDE = range(3)

    def block_copy(kind, chunk, relay=False):
        here = pl.ds(chunk * band_rows, band_rows)
        src = (block_in, left_in, second_ref if relay else left_in)[kind]
        dst = (prior_ref, second_ref, first_ref)[kind]
        return pltpu.make_async_remote_copy(
            src_ref=src.at[here],
            dst_ref=dst.at[here],
            send_sem=block_send.at[kind, chunk],
            recv_sem=block_recv.at[kind, chunk],
            device_id={"blk": (me + 2, me - 2, mate)[kind]},
            device_id_type=MESH,
        )

    def score_copy(kind, c):
        here = pl.ds(c * part, part)
        return pltpu.make_async_remote_copy(
            src_ref=scores.at[1 + kind, :, here],
            dst_ref=scores.at[3 + kind, :, here],
            send_sem=score_send.at[kind, c],
            recv_sem=score_recv.at[kind, c],
            device_id={"blk": me + 1 + kind},
            device_id_type=MESH,
        )

    note = pltpu.make_async_remote_copy(
        src_ref=notes.at[1],
        dst_ref=notes.at[0],
        send_sem=note_send,
        recv_sem=note_recv,
        device_id={"blk": me - 1},
        device_id_type=MESH,
    )
    pl.when(has_left)(lambda: note.start())
    chunks = range(BAND_CHUNKS)
    for c in chunks:
        pl.when(has_next)(lambda c=c: block_copy(AHEAD, c).start())
        pl.when(has_prev)(lambda c=c: block_copy(BEHIND, c).start())
        pl.when(odd == 1)(lambda c=c: block_copy(BESIDE, c).start())

    local = [
        pltpu.make_async_copy(src, dst, local_sem.at[i])
        for i, (src, dst) in enumerate(
            (
                (hidden_in, hidden_ref),
                (context_in, context_ref),
                (weights_in, narrow_ref),
                (left_in, left_ref),
                (block_in, right_ref),
                (table_in, table_ref),
                (grad_in, grad_ref),
            )
        )
    ]
    for copy in local:
        copy.start()

    def edges(ref, number):
        to_left = pltpu.make_async_remote_copy(
            src_ref=ref.at[pl.ds(2, 2)],
            dst_ref=ref.at[pl.ds(width + 2, 2)],
            send_sem=send_sem.at[number, 0],
            recv_sem=recv_sem.at[number, 0],
            device_id={"blk": me - 1},
            device_id_type=MESH,
        )
        to_right = pltpu.make_async_remote_copy(
            src_ref=ref.at[pl.ds(width, 2)],
            dst_ref=ref.at[pl.ds(0, 2)],
            send_sem=send_sem.at[number, 1],
            recv_sem=recv_sem.at[number, 1],
            device_id={"blk": me + 1},
            device_id_type=MESH,
        )
        return to_left, to_right

    def send_edges(ref, number):
        to_left, to_right = edges(ref, number)
        pl.when(has_left)(lambda: to_left.start())
        pl.when(has_right)(lambda: to_right.start())

    def wait_edges(ref, number):
        to_left, to_right = edges(ref, number)
        pl.when(has_left)(lambda: to_left.wait_send())
        pl.when(has_right)(lambda: to_right.wait_send())
        pl.when(has_right)(lambda: to_left.wait_recv())
        pl.when(has_left)(lambda: to_right.wait_recv())

    for copy in local:
        copy.wait()

    @pl.loop(0, height // part)
    def _(c):
        rows = pl.ds(pl.multiple_of(c * part, part), part)
        x0[pl.ds(2, width), rows, pl.ds(0, hd)] = jnp.swapaxes(
            hidden_ref[rows].astype(f32), 0, 1
        ).astype(bf16)

    @pl.loop(0, height // part)
    def _(c):
        rows = pl.ds(pl.multiple_of(c * part, part), part)
        for gate in range(3):
            ctx0[gate, :, rows] = jnp.swapaxes(context_ref[gate, rows].astype(f32), 0, 1)

    deep = narrow_ref.shape[3]
    tail = deep // 16 * 16
    for section in range(2):
        for gate in range(3):
            for k in range(taps):
                weights_ref[section, gate, k, pl.ds(0, tail)] = narrow_ref[section, gate, k, pl.ds(0, tail)]
                rest = narrow_ref[section, gate, k, pl.ds(tail, deep - tail)].astype(f32)
                blank = jnp.zeros((2 * hd - deep, hd), f32)
                weights_ref[section, gate, k, pl.ds(tail, 2 * hd - tail)] = jnp.concatenate(
                    [rest, blank], axis=0
                ).astype(bf16)

    span, lanes = scores.shape[1], scores.shape[3]
    groups = lanes // width

    def score(left, right):
        return jnp.einsum("hxc,hjc->hxj", left, right, preferred_element_type=f32)

    def packed(values):
        parts = [values[:, g * span : (g + 1) * span] for g in range(groups)]
        return jnp.swapaxes(jnp.concatenate(parts, axis=-1), 0, 1).astype(bf16)

    def correlate(c):
        rows = pl.ds(c * part, part)
        right, prior, first = right_ref[rows], prior_ref[rows], first_ref[rows]
        close = notes[0, :, pl.ds(0, width)][None] < 1.5
        scores[0, :, rows] = packed(score(left_ref[rows], jnp.where(offset == 0, right, prior)))
        scores[1, :, rows] = packed(jnp.where(close, score(first, right), score(first, prior)))
        scores[2, :, rows] = packed(score(second_ref[rows], prior))

    pl.when(has_right)(lambda: note.wait_recv())
    bands = height // part
    pieces = part // band_rows
    for c in range(bands + 1):
        if c < bands:

            @pl.when(has_next)
            def _(c=c):
                for chunk in range(c * pieces, (c + 1) * pieces):
                    block_copy(BEHIND, chunk).wait_recv()
                    pl.when(odd == 0)(lambda chunk=chunk: block_copy(BESIDE, chunk, True).start())

        if c >= 1:
            for chunk in range((c - 1) * pieces, c * pieces):
                pl.when(has_prev)(lambda chunk=chunk: block_copy(AHEAD, chunk).wait_recv())
                pl.when(has_right)(lambda chunk=chunk: block_copy(BESIDE, chunk).wait_recv())
            correlate(c - 1)
            pl.when(has_right)(lambda c=c: score_copy(0, c - 1).start())
            pl.when(has_next)(lambda c=c: score_copy(1, c - 1).start())

    for c in range(bands):
        pl.when(has_left)(lambda c=c: score_copy(0, c).wait_recv())
        pl.when(has_prev)(lambda c=c: score_copy(1, c).wait_recv())

    swapped = (offset == 1) | (offset == 3)

    @pl.loop(0, span)
    def _(i):
        even = jnp.where(offset == 3, scores[4, i], scores[0, i])
        other = scores[3, i]
        low = jnp.where(swapped, even, other)
        high = jnp.where(swapped, other, even)
        window = jnp.concatenate([low, high], axis=-1)
        feats = jnp.dot(window, table_ref[i], preferred_element_type=f32).astype(bf16)
        for g in range(groups):
            x0[2 + g * span + i, :, pl.ds(hd, hd)] = feats[:, g * hd : (g + 1) * hd]

    @pl.loop(0, width // part)
    def _(c):
        cols = pl.ds(pl.multiple_of(c * part, part), part)
        feats = x0[pl.ds(2 + c * part, part), :, pl.ds(hd, hd)].astype(f32)
        x1[pl.ds(2, height), cols, pl.ds(hd, hd)] = jnp.swapaxes(feats, 0, 1).astype(bf16)

    send_edges(x0, 0)
    wait_edges(x0, 0)

    def gates(section, x, rx, z, r, context, c):
        total = None
        for k in range(taps):
            w = jnp.concatenate([weights_ref[section, 0, k], weights_ref[section, 1, k]], axis=1)
            term = jnp.dot(flat(x[pl.ds(c * part + k, part)]), w, preferred_element_type=f32)
            total = term if total is None else total + term
        shape = (part,) + x.shape[1:2] + (hd,)
        here = pl.ds(c * part, part)
        z[here] = jax.nn.sigmoid(total[:, :hd].reshape(shape) + context(0, here))
        reset = jax.nn.sigmoid(total[:, hd:].reshape(shape) + context(1, here))
        r[here] = reset
        own = x[pl.ds(c * part + 2, part), :, pl.ds(0, hd)].astype(f32)
        rx[pl.ds(c * part + 2, part)] = (reset * own).astype(bf16)

    def gated(x, rx, first):
        there = pl.ds(first, part)
        return jnp.concatenate([flat(rx[there]), flat(x[there, :, pl.ds(hd, hd)])], axis=1)

    def candidate(section, x, rx, context, c):
        total = None
        for k in range(taps):
            term = jnp.dot(
                gated(x, rx, c * part + k), weights_ref[section, 2, k], preferred_element_type=f32
            )
            total = term if total is None else total + term
        shape = (part,) + x.shape[1:2] + (hd,)
        return jnp.tanh(total.reshape(shape) + context(2, pl.ds(c * part, part)))

    def context_h(gate, here):
        return ctx0[gate, here]

    def context_v(gate, here):
        return context_ref[gate, here].astype(f32)

    @pl.loop(0, width // part)
    def _(c):
        gates(0, x0, rx0, z0, r0, context_h, c)

    send_edges(rx0, 1)
    wait_edges(rx0, 1)

    @pl.loop(0, width // part)
    def _(c):
        here = pl.ds(c * part, part)
        q = candidate(0, x0, rx0, context_h, c)
        q0[here] = q
        z = z0[here]
        own = x0[pl.ds(c * part + 2, part), :, pl.ds(0, hd)].astype(f32)
        blended = (1.0 - z) * own + z * q
        cols = pl.ds(pl.multiple_of(c * part, part), part)
        x1[pl.ds(2, height), cols, pl.ds(0, hd)] = jnp.swapaxes(blended, 0, 1).astype(bf16)

    @pl.loop(0, height // part)
    def _(c):
        gates(1, x1, rx1, z1, r1, context_v, c)

    def deltas(g, z, q, own, dq, dzr, inner):
        dq[inner] = (g * z * (1.0 - q * q)).astype(bf16)
        dzr[inner, :, pl.ds(0, hd)] = (g * (q - own) * z * (1.0 - z)).astype(bf16)

    @pl.loop(0, height // part)
    def _(c):
        here = pl.ds(c * part, part)
        inner = pl.ds(c * part + 2, part)
        q = candidate(1, x1, rx1, context_v, c)
        z = z1[here]
        own = x1[inner, :, pl.ds(0, hd)].astype(f32)
        new_ref[here] = ((1.0 - z) * own + z * q).astype(bf16)
        deltas(grad_ref[here], z, q, own, dq1, dzr1, inner)

    def back_reset(section, x, g, z, r, dq, dzr, c):
        here = pl.ds(c * part, part)
        inner = pl.ds(c * part + 2, part)
        total = None
        for k in range(taps):
            term = lax.dot_general(
                flat(dq[pl.ds(c * part + taps - 1 - k, part)]),
                weights_ref[section, 2, k, pl.ds(0, hd)],
                NT,
                preferred_element_type=f32,
            )
            total = term if total is None else total + term
        total = total.reshape((part,) + x.shape[1:2] + (hd,))
        reset = r[here]
        own = x[inner, :, pl.ds(0, hd)].astype(f32)
        dzr[inner, :, pl.ds(hd, hd)] = (total * own * reset * (1.0 - reset)).astype(bf16)
        r[here] = g[here] * (1.0 - z[here]) + total * reset

    def back_hidden(section, r, dzr, c):
        total = None
        for k in range(taps):
            w = jnp.concatenate(
                [
                    weights_ref[section, 0, k, pl.ds(0, hd)],
                    weights_ref[section, 1, k, pl.ds(0, hd)],
                ],
                axis=1,
            )
            term = lax.dot_general(
                flat(dzr[pl.ds(c * part + taps - 1 - k, part)]), w, NT, preferred_element_type=f32
            )
            total = term if total is None else total + term
        total = total.reshape((part,) + dzr.shape[1:2] + (hd,))
        return r[pl.ds(c * part, part)] + total

    def weight_grads_zr(section, x, dzr, blocks):
        acc[...] = jnp.zeros_like(acc)

        @pl.loop(0, blocks)
        def _(c):
            d = flat(dzr[pl.ds(c * part + 2, part)]).astype(f32).T.astype(bf16)
            for k in range(taps):
                acc[k] += jnp.dot(d, flat(x[pl.ds(c * part + k, part)]), preferred_element_type=f32)

        for k in range(taps):
            for gate in range(2):
                place = (gate * taps + k) * piece
                g_ref[section, pl.ds(place, piece)] = acc[k, pl.ds(gate * hd, hd)].T[:piece]

    def weight_grads_q(section, x, rx, dq, blocks):
        half = pl.ds(0, hd)
        acc[:, half] = jnp.zeros((taps, hd, 2 * hd), f32)

        @pl.loop(0, blocks)
        def _(c):
            d = flat(dq[pl.ds(c * part + 2, part)]).astype(f32).T.astype(bf16)
            for k in range(taps):
                acc[k, half] += jnp.dot(d, gated(x, rx, c * part + k), preferred_element_type=f32)

        for k in range(taps):
            place = (2 * taps + k) * piece
            g_ref[section, pl.ds(place, piece)] = acc[k, half].T[:piece]

    @pl.loop(0, height // part)
    def _(c):
        back_reset(1, x1, grad_ref, z1, r1, dq1, dzr1, c)

    @pl.loop(0, height // part)
    def _(c):
        rows = pl.ds(pl.multiple_of(c * part, part), part)
        g0[:, rows] = jnp.swapaxes(back_hidden(1, r1, dzr1, c), 0, 1)

    @pl.loop(0, width // part)
    def _(c):
        here = pl.ds(c * part, part)
        inner = pl.ds(c * part + 2, part)
        own = x0[inner, :, pl.ds(0, hd)].astype(f32)
        deltas(g0[here], z0[here], q0[here], own, dq0, dzr0, inner)

    total_rows = g_ref.shape[1]
    used = 3 * taps * piece
    if used < total_rows:
        for section in range(2):
            g_ref[section, pl.ds(used, total_rows - used)] = jnp.zeros((total_rows - used, hd), f32)

    depth = len(steps)
    orders = ([0, *range(2, depth), 1], list(range(depth)))
    spans = []
    landing = []
    for order in orders:
        row = [(0, total_rows)]
        places_in = [0]
        for at in order:
            first, length = row[-1]
            share = length // steps[at][2]
            row.append((pl.multiple_of(first + ranks[at] * share, 16), share))
            places_in.append(places_in[-1] + length - share)
        spans.append(row)
        landing.append(places_in)

    def away(section, k, d):
        at = orders[section][k]
        axis, stride, members = steps[at]
        target = lax.rem(partners[at][d][0] // stride, members)
        share = spans[section][k + 1][1]
        return pl.ds(pl.multiple_of(spans[section][k][0] + target * share, 16), share)

    def sum_copies(section, k):
        step = k if k < depth else 2 * depth - 1 - k
        at = orders[section][step]
        own, share = spans[section][step + 1]
        copies = []
        for d in range(1, steps[at][2]):
            if k < depth:
                src = sbuf.at[section, away(section, step, d)]
                dst = rbuf.at[section, pl.ds(landing[section][step] + (d - 1) * share, share)]
            else:
                src = dst = sum_ref.at[section, pl.ds(own, share)]
            place, axis = partners[at][d]
            copies.append(
                pltpu.make_async_remote_copy(
                    src_ref=src,
                    dst_ref=dst,
                    send_sem=sum_send.at[section, k, d],
                    recv_sem=sum_recv.at[section, k, d],
                    device_id={axis: place},
                    device_id_type=MESH,
                )
            )
        return copies

    def begin(section, k):
        copies = sum_copies(section, k)
        for d in range(1, len(copies) + 1):
            if k < depth:
                there = away(section, k, d)
                sbuf[section, there] = g_ref[section, there].astype(bf16)
            copies[d - 1].start()

    def finish(section, k):
        for copy in sum_copies(section, k):
            copy.wait()
        if k < depth:
            keep, share = spans[section][k + 1]
            here = pl.ds(keep, share)
            summed = g_ref[section, here]
            for d in range(1, steps[orders[section][k]][2]):
                landed = rbuf[section, pl.ds(landing[section][k] + (d - 1) * share, share)]
                summed = summed + landed.astype(f32)
            if k == depth - 1:
                sum_ref[section, here] = summed.astype(bf16)
            else:
                g_ref[section, here] = summed

    def turn(section, k):
        if k >= 0:
            finish(section, k)
        if k + 1 < 2 * depth:
            begin(section, k + 1)

    send_edges(dq0, 2)
    weight_grads_zr(1, x1, dzr1, height // part)
    weight_grads_q(1, x1, rx1, dq1, height // part)
    turn(1, -1)
    wait_edges(dq0, 2)

    @pl.loop(0, width // part)
    def _(c):
        back_reset(0, x0, g0, z0, r0, dq0, dzr0, c)

    send_edges(dzr0, 3)
    turn(1, 0)
    weight_grads_q(0, x0, rx0, dq0, width // part)
    turn(1, 1)
    weight_grads_zr(0, x0, dzr0, width // part)
    turn(0, -1)
    turn(1, 2)
    wait_edges(dzr0, 3)

    @pl.loop(0, width // part)
    def _(c):
        cols = pl.ds(pl.multiple_of(c * part, part), part)
        hidden_back_ref[:, cols] = jnp.swapaxes(back_hidden(0, r0, dzr0, c), 0, 1)

    for k in range(2 * depth):
        if k + 3 < 2 * depth:
            turn(1, k + 3)
        turn(0, k)

    pl.when(has_left)(lambda: note.wait_send())
    for c in chunks:
        pl.when(has_next)(lambda c=c: block_copy(AHEAD, c).wait_send())
        pl.when(has_prev)(lambda c=c: block_copy(BEHIND, c).wait_send())
        pl.when((odd == 1) | has_next)(lambda c=c: block_copy(BESIDE, c).wait_send())
    for c in range(bands):
        pl.when(has_right)(lambda c=c: score_copy(0, c).wait_send())
        pl.when(has_next)(lambda c=c: score_copy(1, c).wait_send())


def core(offset, block, left, table, hidden, context, weights, hidden_grad, pairs, count, piece, sum_rows):
    height, width, hd = hidden.shape
    taps = weights.shape[2]
    bf16, f32 = jnp.bfloat16, jnp.float32
    vmem = pl.BlockSpec(memory_space=pltpu.VMEM)
    anywhere = pl.BlockSpec(memory_space=pl.ANY)
    steps = sum_steps(pairs, count)
    narrow = weights.shape
    lanes = hd

    def held(values):
        return pltpu.VMEM(values.shape, values.dtype)

    across = (width, height, hd)
    down = (height, width, hd)

    def padded(shape, wide):
        return pltpu.VMEM((shape[0] + 4, shape[1], wide * hd), bf16)

    return pl.pallas_call(
        functools.partial(core_kernel, count, piece, steps),
        out_shape=(
            jax.ShapeDtypeStruct(hidden.shape, bf16),
            jax.ShapeDtypeStruct(hidden.shape, f32),
            jax.ShapeDtypeStruct((2, sum_rows, hd), bf16),
        ),
        in_specs=[pl.BlockSpec(memory_space=pltpu.SMEM)] + [anywhere] * 7,
        out_specs=(vmem,) * 3,
        scratch_shapes=[
            held(block),
            held(block),
            held(left),
            held(left),
            held(left),
            pltpu.VMEM((5, width * width // lanes, height, lanes), bf16),
            pltpu.VMEM((2, width, lanes), f32),
            held(table),
            held(hidden),
            held(context),
            held(weights),
            held(hidden_grad),
            pltpu.VMEM(narrow[:3] + (2 * hd, hd), bf16),
            pltpu.VMEM((2, sum_rows, hd), f32),
            pltpu.VMEM((2, sum_rows, hd), bf16),
            pltpu.VMEM((2, sum_rows, hd), bf16),
            padded(across, 2),
            padded(down, 2),
            padded(across, 1),
            padded(down, 1),
            padded(across, 1),
            padded(down, 1),
            padded(across, 2),
            padded(down, 2),
            pltpu.VMEM((3,) + across, f32),
            pltpu.VMEM(across, f32),
            pltpu.VMEM(across, f32),
            pltpu.VMEM(across, f32),
            pltpu.VMEM(down, f32),
            pltpu.VMEM(down, f32),
            pltpu.VMEM(across, f32),
            pltpu.VMEM((taps, 2 * hd, 2 * hd), f32),
            pltpu.SemaphoreType.DMA((4, 2)),
            pltpu.SemaphoreType.DMA((4, 2)),
            pltpu.SemaphoreType.DMA((3, BAND_CHUNKS)),
            pltpu.SemaphoreType.DMA((3, BAND_CHUNKS)),
            pltpu.SemaphoreType.DMA((2, height // 16)),
            pltpu.SemaphoreType.DMA((2, height // 16)),
            pltpu.SemaphoreType.DMA(()),
            pltpu.SemaphoreType.DMA(()),
            pltpu.SemaphoreType.DMA((2, 2 * len(steps), 8)),
            pltpu.SemaphoreType.DMA((2, 2 * len(steps), 8)),
            pltpu.SemaphoreType.DMA((7,)),
        ],
        compiler_params=pltpu.CompilerParams(
            collective_id=0, has_side_effects=True, vmem_limit_bytes=58 * 1024 * 1024
        ),
        name="core",
    )(offset, block, left, table, hidden, context, weights, hidden_grad)


def on_device(left_feats, right_feats, offsets, hidden, context, gru_weights, hidden_grad):
    left_block = left_feats[0]
    right_block = right_feats[0]
    column_count = left_block.shape[1]
    table = lookup_table(column_count, LEVELS, RADIUS) / math.sqrt(left_block.shape[-1])
    hd = gru_weights.shape[-1]
    table = packed_table(table, hd)
    table = jnp.asarray(table, jnp.bfloat16)
    pairs, blks = lax.axis_size("pair"), lax.axis_size("blk")
    shape = gru_weights.shape
    piece = -(-shape[3] // 8) * 8
    used = math.prod(shape[1:3]) * piece
    new_hidden, hidden_back, summed = core(
        offsets,
        right_block,
        left_block,
        table,
        hidden[0],
        context[0],
        gru_weights,
        hidden_grad[0],
        pairs,
        blks,
        piece,
        sum_rows_count(used, pairs * blks),
    )
    summed = summed[:, :used].reshape(shape[:3] + (piece, hd))
    grad_stack = summed[:, :, :, : shape[3]].astype(jnp.float32)
    return (new_hidden[None], grad_stack, hidden_back[None])


def solution(mesh):
    placed = (
        P("pair", None, "blk", None),
        P("pair", None, "blk", None),
        P("blk"),
        P("pair", None, "blk", None),
        P("pair", None, None, "blk", None),
        P(),
        P("pair", None, "blk", None),
    )
    return jax.shard_map(
        on_device,
        mesh=mesh,
        in_specs=placed,
        out_specs=(P("pair", None, "blk", None), P(), P("pair", None, "blk", None)),
        check_vma=False,
    )
```

```python
import functools
import math

import jax
import jax.numpy as jnp
import numpy as np
from jax import lax
from jax.experimental import pallas as pl
from jax.experimental.pallas import tpu as pltpu
from jax.sharding import PartitionSpec as P

LEVELS = 4
RADIUS = 4


def lookup_table(column_count, level_count, radius_len):
    tap_count = 2 * radius_len + 1
    lookup = np.zeros((column_count, 2 * column_count, level_count * tap_count), np.float32)
    positions = np.arange(column_count)
    for level_id in range(level_count):
        pool_span = 2**level_id
        pooled_cols = 2 * column_count // pool_span
        for tap_id in range(tap_count):
            centre = (positions + column_count // 2) // pool_span + tap_id - radius_len
            inside = (centre >= 0) & (centre < pooled_cols)
            for inner_id in range(pool_span):
                lookup[
                    positions[inside],
                    centre[inside] * pool_span + inner_id,
                    level_id * tap_count + tap_id,
                ] = (
                    1.0 / pool_span
                )
    return lookup


def packed_table(lookup, lanes):
    width, _, feats = lookup.shape
    groups = lanes // width
    span = width // groups
    table = np.zeros((span, 2, groups, width, groups, lanes), np.float32)
    for group in range(groups):
        columns = lookup[group * span : (group + 1) * span].reshape(span, 2, width, feats)
        table[:, :, group, :, group, :feats] = columns
    return table.reshape(span, 2 * lanes, groups * lanes)


MESH = pl.DeviceIdType.MESH
BAND_CHUNKS = 8
IN_FLIGHT = 2


def sum_steps(pairs, blks):
    steps = []
    for axis, size, most in (("pair", pairs, 2), ("blk", blks, 8)):
        stride = 1
        while stride < size:
            members = min(most, size // stride)
            steps.append((axis, stride, members))
            stride *= members
    return steps


PARCELS = (((1, 0), (1, 1), (1, 2)), ((0, 2), (0, 0)), ((0, 1),))


def sum_orders(depth):
    along = [(at,) for at in range(depth)]
    across = [(0,), *along[2:], (1,)]
    joint = [(0,), (1, 2), *along[3:]]
    return along, along, along


def gate_places(parcels, gate_rows):
    places = {}
    for members, first, _ in parcels:
        for at, member in enumerate(members):
            places[member] = first + at * gate_rows
    return places


def sum_parcels(gate_rows, devices):
    step = devices * 16
    parcels = []
    first = 0
    for members in PARCELS:
        length = -(-len(members) * gate_rows // step) * step
        parcels.append((members, first, length))
        first += length
    return parcels


NT = (((1,), (1,)), ((), ()))


def flat(values):
    return values.reshape(-1, values.shape[-1])


def core_kernel(
    count,
    piece,
    steps,
    parcels,
    offset_ref,
    block_in,
    left_in,
    table_in,
    hidden_in,
    context_in,
    weights_in,
    grad_in,
    new_out,
    hidden_back_out,
    grads_out,
    new_ref,
    hidden_back_ref,
    sum_ref,
    right_ref,
    prior_ref,
    left_ref,
    first_ref,
    second_ref,
    scores,
    notes,
    table_ref,
    hidden_ref,
    context_ref,
    narrow_ref,
    picks,
    grad_ref,
    weights_ref,
    g_ref,
    sbuf,
    rbuf,
    x0,
    x1,
    rx0,
    rx1,
    dq0,
    dq1,
    dzr0,
    dzr1,
    ctx0,
    z0,
    r0,
    q0,
    z1,
    r1,
    g0,
    acc,
    send_sem,
    recv_sem,
    block_send,
    block_recv,
    score_send,
    score_recv,
    note_send,
    note_recv,
    rim_send,
    rim_recv,
    sum_send,
    sum_recv,
    local_sem,
    out_sem,
):
    height, width, hd = hidden_ref.shape
    taps = weights_ref.shape[2]
    me = lax.axis_index("blk")
    has_left = me >= 1
    has_right = me + 1 < count
    bf16, f32 = jnp.bfloat16, jnp.float32
    part = 16

    for ref in (x0, x1, rx0, rx1, dq0, dq1, dzr0, dzr1):
        edge = jnp.zeros((2,) + ref.shape[1:], bf16)
        ref[pl.ds(0, 2)] = edge
        ref[pl.ds(ref.shape[0] - 2, 2)] = edge

    offset = offset_ref[0]
    notes[1] = jnp.full(notes.shape[1:], offset, jnp.int32).astype(f32)

    barrier = pltpu.get_barrier_semaphore()
    position = {"pair": lax.axis_index("pair"), "blk": me}
    orders = sum_orders(len(steps))
    digits = [lax.rem(position[axis] // stride, members) for axis, stride, members in steps]

    def partner(apart):
        places = {}
        for at, d in apart:
            axis, stride, members = steps[at]
            place = places.get(axis, position[axis])
            mask = 1
            while mask < members:
                if d & mask:
                    bit = lax.rem(digits[at] // mask, 2)
                    place = place + stride * mask * (1 - 2 * bit)
                mask *= 2
            places[axis] = place
        return places

    def split(group, d):
        apart = []
        for at in group:
            members = steps[at][2]
            if d % members:
                apart.append((at, d % members))
            d //= members
        return tuple(apart)

    def size(group):
        return math.prod(steps[at][2] for at in group)

    def rank(group):
        total, scale = 0, 1
        for at in group:
            total = total + digits[at] * scale
            scale *= steps[at][2]
        return total

    met = sorted({split(group, d) for order in orders for group in order for d in range(1, size(group))})
    for apart in met:
        pl.semaphore_signal(barrier, inc=1, device_id=partner(apart), device_id_type=MESH)
    has_next = me + 2 < count
    has_prev = me >= 2
    expected = len(met)
    for present, shift in ((has_left, -1), (has_right, 1), (has_prev, -2), (has_next, 2)):

        @pl.when(present)
        def _(shift=shift):
            pl.semaphore_signal(barrier, inc=1, device_id={"blk": me + shift}, device_id_type=MESH)

        expected = expected + present.astype(jnp.int32)
    pl.semaphore_wait(barrier, expected)

    odd = lax.rem(me, 2)
    mate = me + 1 - 2 * odd
    band_rows = height // BAND_CHUNKS

    AHEAD, BEHIND, BESIDE = range(3)

    def block_copy(kind, chunk, relay=False):
        here = pl.ds(chunk * band_rows, band_rows)
        src = (block_in, left_in, second_ref if relay else left_in)[kind]
        dst = (prior_ref, second_ref, first_ref)[kind]
        return pltpu.make_async_remote_copy(
            src_ref=src.at[here],
            dst_ref=dst.at[here],
            send_sem=block_send.at[kind, chunk],
            recv_sem=block_recv.at[kind, chunk],
            device_id={"blk": (me + 2, me - 2, mate)[kind]},
            device_id_type=MESH,
        )

    def score_copy(kind, c):
        here = pl.ds(pl.multiple_of(c * part, part), part)
        return pltpu.make_async_remote_copy(
            src_ref=scores.at[1 + kind, :, here],
            dst_ref=scores.at[3 + kind, :, here],
            send_sem=score_send.at[kind, c],
            recv_sem=score_recv.at[kind, c],
            device_id={"blk": me + 1 + kind},
            device_id_type=MESH,
        )

    note = pltpu.make_async_remote_copy(
        src_ref=notes.at[1],
        dst_ref=notes.at[0],
        send_sem=note_send,
        recv_sem=note_recv,
        device_id={"blk": me - 1},
        device_id_type=MESH,
    )
    pl.when(has_left)(lambda: note.start())
    bands = height // part
    pieces = part // band_rows

    def outgoing(chunk, act):
        pl.when(has_next)(lambda: act(block_copy(AHEAD, chunk)))
        pl.when(has_prev)(lambda: act(block_copy(BEHIND, chunk)))
        pl.when(odd == 1)(lambda: act(block_copy(BESIDE, chunk)))

    def start_blocks(chunk):
        outgoing(chunk, lambda copy: copy.start())

    def sent_blocks(chunk):
        outgoing(chunk, lambda copy: copy.wait_send())

    for chunk in range(IN_FLIGHT):
        start_blocks(chunk)

    local = [
        pltpu.make_async_copy(src, dst, local_sem.at[i])
        for i, (src, dst) in enumerate(
            (
                (hidden_in, hidden_ref),
                (context_in, context_ref),
                (weights_in, narrow_ref),
                (left_in, left_ref),
                (block_in, right_ref),
                (table_in, table_ref),
                (grad_in, grad_ref),
            )
        )
    ]
    for copy in local:
        copy.start()

    def edges(ref, number, c=None):
        rows = slice(None) if c is None else pl.ds(pl.multiple_of(c * part, part), part)
        sems = (number,) if c is None else (number, c)
        to_left = pltpu.make_async_remote_copy(
            src_ref=ref.at[pl.ds(2, 2), rows],
            dst_ref=ref.at[pl.ds(width + 2, 2), rows],
            send_sem=(send_sem if c is None else rim_send).at[(*sems, 0)],
            recv_sem=(recv_sem if c is None else rim_recv).at[(*sems, 0)],
            device_id={"blk": me - 1},
            device_id_type=MESH,
        )
        to_right = pltpu.make_async_remote_copy(
            src_ref=ref.at[pl.ds(width, 2), rows],
            dst_ref=ref.at[pl.ds(0, 2), rows],
            send_sem=(send_sem if c is None else rim_send).at[(*sems, 1)],
            recv_sem=(recv_sem if c is None else rim_recv).at[(*sems, 1)],
            device_id={"blk": me + 1},
            device_id_type=MESH,
        )
        return to_left, to_right

    def send_edges(ref, number, c=None):
        to_left, to_right = edges(ref, number, c)
        pl.when(has_left)(lambda: to_left.start())
        pl.when(has_right)(lambda: to_right.start())

    def wait_edges(ref, number, c=None):
        to_left, to_right = edges(ref, number, c)
        pl.when(has_left)(lambda: to_left.wait_send())
        pl.when(has_right)(lambda: to_right.wait_send())
        pl.when(has_right)(lambda: to_left.wait_recv())
        pl.when(has_left)(lambda: to_right.wait_recv())

    @pl.when(me < 2)
    def _():
        prior_ref[...] = jnp.zeros(prior_ref.shape, bf16)
        scores[4] = jnp.zeros(scores.shape[1:], bf16)

    @pl.when(me < 1)
    def _():
        scores[3] = jnp.zeros(scores.shape[1:], bf16)

    def prepare(c):
        rows = pl.ds(pl.multiple_of(c * part, part), part)
        x0[pl.ds(2, width), rows, pl.ds(0, hd)] = jnp.swapaxes(
            hidden_ref[rows].astype(f32), 0, 1
        ).astype(bf16)
        for gate in range(3):
            ctx0[gate, :, rows] = jnp.swapaxes(context_ref[gate, rows].astype(f32), 0, 1)

    mixed = narrow_ref.shape[2]
    channel = lax.broadcasted_iota(jnp.int32, (4 * hd, mixed), 0)
    column = lax.broadcasted_iota(jnp.int32, (4 * hd, mixed), 1)
    wanted = jnp.where(channel < 2 * hd, 2 * channel, 2 * channel - 4 * hd + 1)
    inside = lax.rem(channel, 2 * hd) < mixed // 2
    picks[...] = jnp.where((wanted == column) & inside, 1.0, 0.0).astype(bf16)

    def sort_weights(gate):
        @pl.loop(0, taps)
        def _(k):
            sorted_rows = jnp.dot(picks[...], narrow_ref[gate, k], preferred_element_type=f32).astype(bf16)
            weights_ref[0, gate, k] = sorted_rows[: 2 * hd]
            weights_ref[1, gate, k] = sorted_rows[2 * hd :]

    span, lanes = scores.shape[1], scores.shape[3]
    groups = lanes // width

    def score(left, right):
        return jnp.einsum("hxc,hjc->hxj", left, right, preferred_element_type=f32)

    def packed(values):
        parts = [values[:, g * span : (g + 1) * span] for g in range(groups)]
        return jnp.swapaxes(jnp.concatenate(parts, axis=-1), 0, 1).astype(bf16)

    def correlate(c):
        rows = pl.ds(pl.multiple_of(c * part, part), part)
        right, prior, first = right_ref[rows], prior_ref[rows], first_ref[rows]
        close = notes[0, :, pl.ds(0, width)][None] < 1.5
        scores[0, :, rows] = packed(score(left_ref[rows], jnp.where(offset == 0, right, prior)))
        scores[1, :, rows] = packed(jnp.where(close, score(first, right), score(first, prior)))
        scores[2, :, rows] = packed(score(second_ref[rows], prior))

    swapped = (offset == 1) | (offset == 3)

    def pass_on(chunk):
        @pl.when(has_next)
        def _():
            block_copy(BEHIND, chunk).wait_recv()
            pl.when(odd == 0)(lambda: block_copy(BESIDE, chunk, True).start())

        sent_blocks(chunk)
        pl.when(chunk + IN_FLIGHT < BAND_CHUNKS)(lambda: start_blocks(chunk + IN_FLIGHT))

    def meet(c):
        for chunk in [c * pieces + p for p in range(pieces)]:
            pl.when(has_prev)(lambda: block_copy(AHEAD, chunk).wait_recv())
            pl.when(has_right)(lambda: block_copy(BESIDE, chunk).wait_recv())
        correlate(c)
        pl.when(has_right)(lambda: score_copy(0, c).start())
        pl.when(has_next)(lambda: score_copy(1, c).start())

    def features(c):
        pl.when(has_left)(lambda: score_copy(0, c).wait_recv())
        pl.when(has_prev)(lambda: score_copy(1, c).wait_recv())
        rows = pl.ds(pl.multiple_of(c * part, part), part)
        even = jnp.where(offset == 3, scores[4, :, rows], scores[0, :, rows])
        other = scores[3, :, rows]
        low = jnp.where(swapped, even, other)
        high = jnp.where(swapped, other, even)
        window = jnp.concatenate([low, high], axis=-1)
        feats = jnp.einsum("ihj,ijf->ihf", window, table_ref[...], preferred_element_type=f32)
        feats = jnp.concatenate([feats[:, :, g * hd : (g + 1) * hd] for g in range(groups)], axis=0)
        x0[pl.ds(2, width), rows, pl.ds(hd, hd)] = feats.astype(bf16)
        x1[pl.ds(2 + c * part, part), :, pl.ds(hd, hd)] = jnp.swapaxes(feats, 0, 1).astype(bf16)
        send_edges(x0, 0, c)

    def view(section, c):
        if section:
            here = (pl.ds(c * part, part),)
            inner = (pl.ds(c * part + 2, part),)
            return here, inner, lambda k: (pl.ds(c * part + k, part), slice(None))
        rows = pl.ds(pl.multiple_of(c * part, part), part)
        return (slice(None), rows), (pl.ds(2, width), rows), lambda k: (pl.ds(k, width), rows)

    def gates(section, x, rx, z, r, context, c):
        here, inner, at = view(section, c)
        total = None
        for k in range(taps):
            w = jnp.concatenate([weights_ref[section, 0, k], weights_ref[section, 1, k]], axis=1)
            term = jnp.dot(flat(x[at(k)]), w, preferred_element_type=f32)
            total = term if total is None else total + term
        own = x[(*at(2), pl.ds(0, hd))].astype(f32)
        z[here] = jax.nn.sigmoid(total[:, :hd].reshape(own.shape) + context(0, here))
        reset = jax.nn.sigmoid(total[:, hd:].reshape(own.shape) + context(1, here))
        r[here] = reset
        rx[inner] = (reset * own).astype(bf16)

    def gated(x, rx, there):
        return jnp.concatenate([flat(rx[there]), flat(x[(*there, pl.ds(hd, hd))])], axis=1)

    def candidate(section, x, rx, context, c):
        here, _, at = view(section, c)
        total = None
        for k in range(taps):
            term = jnp.dot(gated(x, rx, at(k)), weights_ref[section, 2, k], preferred_element_type=f32)
            total = term if total is None else total + term
        near = context(2, here)
        return jnp.tanh(total.reshape(near.shape) + near)

    def context_h(gate, here):
        return ctx0[(gate, *here)]

    def context_v(gate, here):
        return context_ref[(gate, *here)].astype(f32)

    def reset_h(c):
        wait_edges(x0, 0, c)
        gates(0, x0, rx0, z0, r0, context_h, c)
        send_edges(rx0, 1, c)

    def blend_h(c):
        wait_edges(rx0, 1, c)
        here, inner, _ = view(0, c)
        q = candidate(0, x0, rx0, context_h, c)
        q0[here] = q
        z = z0[here]
        own = x0[(*inner, pl.ds(0, hd))].astype(f32)
        blended = (1.0 - z) * own + z * q
        x1[pl.ds(2 + c * part, part), :, pl.ds(0, hd)] = jnp.swapaxes(blended, 0, 1).astype(bf16)

    def arrived(t):
        @pl.when(t == 0)
        def _():
            for copy in local[:5]:
                copy.wait()
            pl.when(has_right)(lambda: note.wait_recv())

        pl.when(t == 1)(lambda: local[5].wait())

    def within(first, last, stage):
        return lambda t: pl.when((t >= first) & (t < last))(lambda: stage(t - first))

    stages = [
        [within(4, bands + 4, blend_h), within(3, bands + 3, reset_h)],
        [within(2, bands + 2, features)],
        [within(1, bands + 1, meet)],
        [arrived, within(0, bands, prepare), within(0, 3, sort_weights)],
    ]

    @pl.loop(0, bands + 4)
    def _(t):
        for at, group in enumerate(stages):
            for stage in group:
                stage(t)
            for p in range(at * pieces // len(stages), (at + 1) * pieces // len(stages)):
                pl.when(t < bands)(lambda: pass_on(t * pieces + p))

    local[6].wait()

    @pl.loop(0, height // part)
    def _(c):
        gates(1, x1, rx1, z1, r1, context_v, c)

    def deltas(g, z, q, own, dq, dzr, inner):
        dq[inner] = (g * z * (1.0 - q * q)).astype(bf16)
        dzr[inner, :, pl.ds(0, hd)] = (g * (q - own) * z * (1.0 - z)).astype(bf16)

    @pl.loop(0, height // part)
    def _(c):
        here = pl.ds(c * part, part)
        inner = pl.ds(c * part + 2, part)
        q = candidate(1, x1, rx1, context_v, c)
        z = z1[here]
        own = x1[inner, :, pl.ds(0, hd)].astype(f32)
        new_ref[here] = ((1.0 - z) * own + z * q).astype(bf16)
        deltas(grad_ref[here], z, q, own, dq1, dzr1, inner)

    def back_reset(section, x, g, z, r, dq, dzr, c):
        here = pl.ds(c * part, part)
        inner = pl.ds(c * part + 2, part)
        total = None
        for k in range(taps):
            term = lax.dot_general(
                flat(dq[pl.ds(c * part + taps - 1 - k, part)]),
                weights_ref[section, 2, k, pl.ds(0, hd)],
                NT,
                preferred_element_type=f32,
            )
            total = term if total is None else total + term
        total = total.reshape((part,) + x.shape[1:2] + (hd,))
        reset = r[here]
        own = x[inner, :, pl.ds(0, hd)].astype(f32)
        dzr[inner, :, pl.ds(hd, hd)] = (total * own * reset * (1.0 - reset)).astype(bf16)
        r[here] = g[here] * (1.0 - z[here]) + total * reset

    def back_hidden(section, r, dzr, c):
        total = None
        for k in range(taps):
            w = jnp.concatenate(
                [
                    weights_ref[section, 0, k, pl.ds(0, hd)],
                    weights_ref[section, 1, k, pl.ds(0, hd)],
                ],
                axis=1,
            )
            term = lax.dot_general(
                flat(dzr[pl.ds(c * part + taps - 1 - k, part)]), w, NT, preferred_element_type=f32
            )
            total = term if total is None else total + term
        total = total.reshape((part,) + dzr.shape[1:2] + (hd,))
        return r[pl.ds(c * part, part)] + total

    gate_rows = taps * piece
    places = gate_places(parcels, gate_rows)
    for members, first, length in parcels:
        used = len(members) * gate_rows
        if used < length:
            g_ref[pl.ds(first + used, length - used)] = jnp.zeros((length - used, hd), f32)

    def weight_grads(section, gates, blocks, d_ref, taken):
        lanes = pl.ds(gates[0] % 2 * hd, len(gates) * hd)
        rows = pl.ds(0, len(gates) * hd)
        acc[:, rows] = jnp.zeros((taps, len(gates) * hd, 2 * hd), f32)

        @pl.loop(0, blocks)
        def _(c):
            d = flat(d_ref[pl.ds(c * part + 2, part), :, lanes]).astype(f32).T.astype(bf16)
            for k in range(taps):
                acc[k, rows] += jnp.dot(d, taken(c * part + k), preferred_element_type=f32)

        for k in range(taps):
            for at, gate in enumerate(gates):
                place = places[section, gate] + k * piece
                g_ref[pl.ds(place, piece)] = acc[k, pl.ds(at * hd, hd)].T[:piece]

    def plain(x):
        return lambda first: flat(x[pl.ds(first, part)])

    spans = []
    landing = []
    for order, (_, base, total_rows) in zip(orders, parcels):
        row = [(base, total_rows)]
        places_in = [base]
        for group in order:
            first, length = row[-1]
            share = length // size(group)
            row.append((pl.multiple_of(first + rank(group) * share, 16), share))
            places_in.append(places_in[-1] + length - share)
        spans.append(row)
        landing.append(places_in)

    def away(section, step, d):
        group = orders[section][step]
        target, scale = 0, 1
        for at in group:
            axis, stride, members = steps[at]
            there = dict(split(group, d)).get(at, 0)
            place = partner(((at, there),))[axis]
            target = target + lax.rem(place // stride, members) * scale
            scale *= members
        share = spans[section][step + 1][1]
        return pl.ds(pl.multiple_of(spans[section][step][0] + target * share, 16), share)

    def stage_of(section, k):
        depth = len(orders[section])
        step = k if k < depth else 2 * depth - 1 - k
        return depth, step, orders[section][step]

    def begin(section, k):
        depth, step, group = stage_of(section, k)
        own, share = spans[section][step + 1]
        for d in range(1, size(group)):
            if k < depth:
                there = away(section, step, d)
                sbuf[there] = g_ref[there].astype(bf16)
                src = sbuf.at[there]
                dst = rbuf.at[pl.ds(landing[section][step] + (d - 1) * share, share)]
            else:
                src = dst = sum_ref.at[pl.ds(own, share)]
            pltpu.make_async_remote_copy(
                src_ref=src,
                dst_ref=dst,
                send_sem=sum_send.at[section, k],
                recv_sem=sum_recv.at[section, k],
                device_id=partner(split(group, d)),
                device_id_type=MESH,
            ).start()

    def grad_copy(section):
        _, first, length = parcels[section]
        whole = pl.ds(first, length)
        return pltpu.make_async_copy(sum_ref.at[whole], grads_out.at[whole], out_sem.at[2 + section])

    def finish(section, k):
        depth, step, group = stage_of(section, k)
        keep, share = spans[section][step + 1]
        moved = pl.ds(landing[section][step if k < depth else 0], (size(group) - 1) * share)
        for sem in (sum_send, sum_recv):
            ref = rbuf if k < depth else sum_ref
            pltpu.make_async_copy(ref.at[moved], ref.at[moved], sem.at[section, k]).wait()
        if k < depth:
            here = pl.ds(keep, share)
            summed = g_ref[here]
            for d in range(1, size(group)):
                landed = rbuf[pl.ds(landing[section][step] + (d - 1) * share, share)]
                summed = summed + landed.astype(f32)
            if k == depth - 1:
                sum_ref[here] = summed.astype(bf16)
            else:
                g_ref[here] = summed
        elif k == 2 * depth - 1:
            grad_copy(section).start()

    def turn(section, k):
        last = 2 * len(orders[section]) - 1
        if 0 <= k <= last:
            finish(section, k)
        if k < last:
            begin(section, k + 1)

    new_copy = pltpu.make_async_copy(new_ref, new_out, out_sem.at[0])
    new_copy.start()

    @pl.loop(0, height // part)
    def _(c):
        back_reset(1, x1, grad_ref, z1, r1, dq1, dzr1, c)

    blocks_h, blocks_v = width // part, height // part
    weight_grads(1, (0, 1), blocks_v, dzr1, plain(x1))
    weight_grads(1, (2,), blocks_v, dq1, lambda first: gated(x1, rx1, (pl.ds(first, part), slice(None))))
    turn(0, -1)

    @pl.loop(0, height // part)
    def _(c):
        rows = pl.ds(pl.multiple_of(c * part, part), part)
        g0[:, rows] = jnp.swapaxes(back_hidden(1, r1, dzr1, c), 0, 1)

    @pl.loop(0, width // part)
    def _(c):
        here = pl.ds(c * part, part)
        inner = pl.ds(c * part + 2, part)
        own = x0[inner, :, pl.ds(0, hd)].astype(f32)
        deltas(g0[here], z0[here], q0[here], own, dq0, dzr0, inner)

    send_edges(dq0, 0)
    turn(0, 0)
    weight_grads(0, (2,), blocks_h, dq0, lambda first: gated(x0, rx0, (pl.ds(first, part), slice(None))))
    weight_grads(0, (0,), blocks_h, dzr0, plain(x0))
    turn(1, -1)
    wait_edges(dq0, 0)

    @pl.loop(0, width // part)
    def _(c):
        back_reset(0, x0, g0, z0, r0, dq0, dzr0, c)

    send_edges(dzr0, 1)
    turn(0, 1)
    turn(1, 0)
    weight_grads(0, (1,), blocks_h, dzr0, plain(x0))
    turn(2, -1)
    wait_edges(dzr0, 1)

    @pl.loop(0, width // part)
    def _(c):
        cols = pl.ds(pl.multiple_of(c * part, part), part)
        hidden_back_ref[:, cols] = jnp.swapaxes(back_hidden(0, r0, dzr0, c), 0, 1)

    back_copy = pltpu.make_async_copy(hidden_back_ref, hidden_back_out, out_sem.at[1])
    back_copy.start()

    for k in range(2 * len(steps)):
        turn(2, k)
        turn(0, k + 2)
        turn(1, k + 1)

    new_copy.wait()
    back_copy.wait()
    for section in range(len(parcels)):
        grad_copy(section).wait()
    pl.when(has_left)(lambda: note.wait_send())
    for c in range(BAND_CHUNKS):
        pl.when((odd == 0) & has_next)(lambda c=c: block_copy(BESIDE, c, True).wait_send())
    for c in range(bands):
        pl.when(has_right)(lambda c=c: score_copy(0, c).wait_send())
        pl.when(has_next)(lambda c=c: score_copy(1, c).wait_send())


def finish_kernel(
    places, new_in, back_in, sums_in, new_out, back_out, grads_out, new, back, sums, rows, grads, sems
):
    sections, gates = 2, len(places) // 2
    taps, mixed = grads.shape[1:3]
    depth = mixed // sections
    piece = -(-depth // 8) * 8
    load = pltpu.make_async_copy(sums_in, sums, sems.at[0])
    load.start()
    enter = [pltpu.make_async_copy(new_in, new, sems.at[1]), pltpu.make_async_copy(back_in, back, sems.at[2])]
    for copy in enter:
        copy.start()
    load.wait()
    for copy in enter:
        copy.wait()
    through = [pltpu.make_async_copy(new, new_out, sems.at[1]), pltpu.make_async_copy(back, back_out, sems.at[2])]
    for copy in through:
        copy.start()
    rows[...] = sums[...].astype(jnp.float32)
    for gate in range(gates):
        for tap in range(taps):
            for section in range(sections):
                taken = rows[pl.ds(places[section, gate] + tap * piece, depth)]
                grads[gate, tap, pl.ds(section, depth, stride=sections)] = taken
        through.append(pltpu.make_async_copy(grads.at[gate], grads_out.at[gate], sems.at[3 + gate]))
        through[-1].start()
    for copy in through:
        copy.wait()


def finished(new_hidden, hidden_back, sums, places, shape):
    anywhere = pl.BlockSpec(memory_space=pl.ANY)
    f32 = jnp.float32
    return pl.pallas_call(
        functools.partial(finish_kernel, places),
        out_shape=(
            jax.ShapeDtypeStruct(new_hidden.shape, new_hidden.dtype),
            jax.ShapeDtypeStruct(hidden_back.shape, hidden_back.dtype),
            jax.ShapeDtypeStruct(shape, f32),
        ),
        in_specs=[anywhere] * 3,
        out_specs=(anywhere,) * 3,
        scratch_shapes=[
            pltpu.VMEM(new_hidden.shape, new_hidden.dtype),
            pltpu.VMEM(hidden_back.shape, hidden_back.dtype),
            pltpu.VMEM(sums.shape, sums.dtype),
            pltpu.VMEM(sums.shape, f32),
            pltpu.VMEM(shape, f32),
            pltpu.SemaphoreType.DMA((3 + shape[0],)),
        ],
        compiler_params=pltpu.CompilerParams(vmem_limit_bytes=58 * 1024 * 1024),
        name="finish",
    )(new_hidden, hidden_back, sums)


def core(offset, block, left, table, hidden, context, weights, hidden_grad, pairs, count, piece):
    height, width, hd = hidden.shape
    taps = weights.shape[1]
    bf16, f32 = jnp.bfloat16, jnp.float32
    anywhere = pl.BlockSpec(memory_space=pl.ANY)
    steps = sum_steps(pairs, count)
    lanes = hd
    gate_rows = taps * piece
    parcels = sum_parcels(gate_rows, pairs * count)
    sum_rows = sum(length for _, _, length in parcels)

    def held(values):
        return pltpu.VMEM(values.shape, values.dtype)

    across = (width, height, hd)
    down = (height, width, hd)

    def padded(shape, wide):
        return pltpu.VMEM((shape[0] + 4, shape[1], wide * hd), bf16)

    return pl.pallas_call(
        functools.partial(core_kernel, count, piece, steps, parcels),
        out_shape=(
            jax.ShapeDtypeStruct(hidden.shape, bf16),
            jax.ShapeDtypeStruct(hidden.shape, f32),
            jax.ShapeDtypeStruct((sum_rows, hd), bf16),
        ),
        in_specs=[pl.BlockSpec(memory_space=pltpu.SMEM)] + [anywhere] * 7,
        out_specs=(anywhere,) * 3,
        scratch_shapes=[
            held(hidden),
            pltpu.VMEM(hidden.shape, f32),
            pltpu.VMEM((sum_rows, hd), bf16),
            held(block),
            held(block),
            held(left),
            held(left),
            held(left),
            pltpu.VMEM((5, width * width // lanes, height, lanes), bf16),
            pltpu.VMEM((2, width, lanes), f32),
            held(table),
            held(hidden),
            held(context),
            held(weights),
            pltpu.VMEM((4 * hd, weights.shape[2]), bf16),
            held(hidden_grad),
            pltpu.VMEM((2, 3, taps, 2 * hd, hd), bf16),
            pltpu.VMEM((sum_rows, hd), f32),
            pltpu.VMEM((sum_rows, hd), bf16),
            pltpu.VMEM((sum_rows, hd), bf16),
            padded(across, 2),
            padded(down, 2),
            padded(across, 1),
            padded(down, 1),
            padded(across, 1),
            padded(down, 1),
            padded(across, 2),
            padded(down, 2),
            pltpu.VMEM((3,) + across, f32),
            pltpu.VMEM(across, f32),
            pltpu.VMEM(across, f32),
            pltpu.VMEM(across, f32),
            pltpu.VMEM(down, f32),
            pltpu.VMEM(down, f32),
            pltpu.VMEM(across, f32),
            pltpu.VMEM((taps, 2 * hd, 2 * hd), f32),
            pltpu.SemaphoreType.DMA((2, 2)),
            pltpu.SemaphoreType.DMA((2, 2)),
            pltpu.SemaphoreType.DMA((3, BAND_CHUNKS)),
            pltpu.SemaphoreType.DMA((3, BAND_CHUNKS)),
            pltpu.SemaphoreType.DMA((2, height // 16)),
            pltpu.SemaphoreType.DMA((2, height // 16)),
            pltpu.SemaphoreType.DMA(()),
            pltpu.SemaphoreType.DMA(()),
            pltpu.SemaphoreType.DMA((2, height // 16, 2)),
            pltpu.SemaphoreType.DMA((2, height // 16, 2)),
            pltpu.SemaphoreType.DMA((3, 2 * len(steps))),
            pltpu.SemaphoreType.DMA((3, 2 * len(steps))),
            pltpu.SemaphoreType.DMA((7,)),
            pltpu.SemaphoreType.DMA((5,)),
        ],
        compiler_params=pltpu.CompilerParams(
            collective_id=0, has_side_effects=True, vmem_limit_bytes=58 * 1024 * 1024
        ),
        name="core",
    )(offset, block, left, table, hidden, context, weights, hidden_grad)


def on_device(left_feats, right_feats, offsets, hidden, context, gru_weights, hidden_grad):
    left_block = left_feats[0]
    right_block = right_feats[0]
    column_count = left_block.shape[1]
    table = lookup_table(column_count, LEVELS, RADIUS) / math.sqrt(left_block.shape[-1])
    hd = gru_weights.shape[-1]
    table = packed_table(table, hd)
    table = jnp.asarray(table, jnp.bfloat16)
    pairs, blks = lax.axis_size("pair"), lax.axis_size("blk")
    shape = gru_weights.shape
    piece = -(-shape[3] // 8) * 8
    gate_rows = shape[2] * piece
    mixed = shape[1:3] + (shape[0] * shape[3], hd)
    new_hidden, hidden_back, sums = core(
        offsets,
        right_block,
        left_block,
        table,
        hidden[0],
        context[0],
        jnp.transpose(gru_weights, (1, 2, 3, 0, 4)).reshape(mixed),
        hidden_grad[0],
        pairs,
        blks,
        piece,
    )
    places = gate_places(sum_parcels(gate_rows, pairs * blks), gate_rows)
    new_hidden, hidden_back, grads = finished(new_hidden, hidden_back, sums, places, mixed)
    grads = grads.reshape(shape[1:4] + (shape[0], hd))
    return (new_hidden[None], jnp.transpose(grads, (3, 0, 1, 2, 4)), hidden_back[None])


def solution(mesh):
    placed = (
        P("pair", None, "blk", None),
        P("pair", None, "blk", None),
        P("blk"),
        P("pair", None, "blk", None),
        P("pair", None, None, "blk", None),
        P(),
        P("pair", None, "blk", None),
    )
    return jax.shard_map(
        on_device,
        mesh=mesh,
        in_specs=placed,
        out_specs=(P("pair", None, "blk", None), P(), P("pair", None, "blk", None)),
        check_vma=False,
    )
```

```python
import functools
import math

import jax
import jax.numpy as jnp
import numpy as np
from jax import lax
from jax.experimental import pallas as pl
from jax.experimental.pallas import tpu as pltpu
from jax.sharding import PartitionSpec as P

LEVELS = 4
RADIUS = 4


def lookup_table(column_count, level_count, radius_len):
    tap_count = 2 * radius_len + 1
    lookup = np.zeros((column_count, 2 * column_count, level_count * tap_count), np.float32)
    positions = np.arange(column_count)
    for level_id in range(level_count):
        pool_span = 2**level_id
        pooled_cols = 2 * column_count // pool_span
        for tap_id in range(tap_count):
            centre = (positions + column_count // 2) // pool_span + tap_id - radius_len
            inside = (centre >= 0) & (centre < pooled_cols)
            for inner_id in range(pool_span):
                lookup[
                    positions[inside],
                    centre[inside] * pool_span + inner_id,
                    level_id * tap_count + tap_id,
                ] = (
                    1.0 / pool_span
                )
    return lookup


def packed_table(lookup, lanes):
    width, _, feats = lookup.shape
    groups = lanes // width
    span = width // groups
    table = np.zeros((span, 2, groups, width, groups, lanes), np.float32)
    for group in range(groups):
        columns = lookup[group * span : (group + 1) * span].reshape(span, 2, width, feats)
        table[:, :, group, :, group, :feats] = columns
    return table.reshape(span, 2 * lanes, groups * lanes)


MESH = pl.DeviceIdType.MESH
BAND_CHUNKS = 8
IN_FLIGHT = 2


def sum_steps(pairs, blks):
    steps = []
    for axis, size, most in (("pair", pairs, 2), ("blk", blks, 8)):
        stride = 1
        while stride < size:
            members = min(most, size // stride)
            steps.append((axis, stride, members))
            stride *= members
    return steps


def sum_orders(depth):
    along = [(at,) for at in range(depth)]
    return along, along, along


def sum_layout(gate_rows, devices):
    step = devices * 16
    whole = -(-3 * gate_rows // step) * step
    places = {(1, gate): gate * gate_rows for gate in range(3)}
    ready = 2 * gate_rows // step * step
    if ready:
        late = whole + 2 * gate_rows
    else:
        ready = -(-2 * gate_rows // step) * step
        late = whole + ready
    places.update({(0, 2): whole, (0, 0): whole + gate_rows, (0, 1): late})
    rest = -(-(late + gate_rows - whole - ready) // step) * step
    parcels = ((0, whole), (whole, ready), (whole + ready, rest))
    blanks = []
    at = 0
    for first in sorted(places.values()) + [whole + ready + rest]:
        if first > at:
            blanks.append((at, first - at))
        at = first + gate_rows
    return places, parcels, blanks


NT = (((1,), (1,)), ((), ()))


def flat(values):
    return values.reshape(-1, values.shape[-1])


def core_kernel(
    count,
    piece,
    steps,
    layout,
    offset_ref,
    block_in,
    left_in,
    table_in,
    hidden_in,
    context_in,
    weights_in,
    grad_in,
    new_out,
    hidden_back_out,
    grads_out,
    new_ref,
    hidden_back_ref,
    sum_ref,
    right_ref,
    prior_ref,
    left_ref,
    first_ref,
    second_ref,
    scores,
    notes,
    table_ref,
    hidden_ref,
    context_ref,
    narrow_ref,
    picks,
    grad_ref,
    weights_ref,
    g_ref,
    sbuf,
    rbuf,
    x0,
    x1,
    rx0,
    rx1,
    dq0,
    dq1,
    dzr0,
    dzr1,
    ctx0,
    z0,
    r0,
    q0,
    z1,
    r1,
    g0,
    acc,
    send_sem,
    recv_sem,
    block_send,
    block_recv,
    score_send,
    score_recv,
    note_send,
    note_recv,
    rim_send,
    rim_recv,
    sum_send,
    sum_recv,
    local_sem,
    out_sem,
):
    height, width, hd = hidden_ref.shape
    taps = weights_ref.shape[2]
    me = lax.axis_index("blk")
    has_left = me >= 1
    has_right = me + 1 < count
    bf16, f32 = jnp.bfloat16, jnp.float32
    part = 16

    for ref in (x0, x1, rx0, rx1, dq0, dq1, dzr0, dzr1):
        edge = jnp.zeros((2,) + ref.shape[1:], bf16)
        ref[pl.ds(0, 2)] = edge
        ref[pl.ds(ref.shape[0] - 2, 2)] = edge

    offset = offset_ref[0]
    notes[1] = jnp.full(notes.shape[1:], offset, jnp.int32).astype(f32)

    barrier = pltpu.get_barrier_semaphore()
    position = {"pair": lax.axis_index("pair"), "blk": me}
    orders = sum_orders(len(steps))
    digits = [lax.rem(position[axis] // stride, members) for axis, stride, members in steps]

    def partner(apart):
        places = {}
        for at, d in apart:
            axis, stride, members = steps[at]
            place = places.get(axis, position[axis])
            mask = 1
            while mask < members:
                if d & mask:
                    bit = lax.rem(digits[at] // mask, 2)
                    place = place + stride * mask * (1 - 2 * bit)
                mask *= 2
            places[axis] = place
        return places

    def split(group, d):
        apart = []
        for at in group:
            members = steps[at][2]
            if d % members:
                apart.append((at, d % members))
            d //= members
        return tuple(apart)

    def size(group):
        return math.prod(steps[at][2] for at in group)

    def rank(group):
        total, scale = 0, 1
        for at in group:
            total = total + digits[at] * scale
            scale *= steps[at][2]
        return total

    met = sorted({split(group, d) for order in orders for group in order for d in range(1, size(group))})
    for apart in met:
        pl.semaphore_signal(barrier, inc=1, device_id=partner(apart), device_id_type=MESH)
    has_next = me + 2 < count
    has_prev = me >= 2
    expected = len(met)
    for present, shift in ((has_left, -1), (has_right, 1), (has_prev, -2), (has_next, 2)):

        @pl.when(present)
        def _(shift=shift):
            pl.semaphore_signal(barrier, inc=1, device_id={"blk": me + shift}, device_id_type=MESH)

        expected = expected + present.astype(jnp.int32)
    pl.semaphore_wait(barrier, expected)

    odd = lax.rem(me, 2)
    mate = me + 1 - 2 * odd
    band_rows = height // BAND_CHUNKS

    AHEAD, BEHIND, BESIDE = range(3)

    def block_copy(kind, chunk, relay=False):
        here = pl.ds(chunk * band_rows, band_rows)
        src = (block_in, left_in, second_ref if relay else left_in)[kind]
        dst = (prior_ref, second_ref, first_ref)[kind]
        return pltpu.make_async_remote_copy(
            src_ref=src.at[here],
            dst_ref=dst.at[here],
            send_sem=block_send.at[kind, chunk],
            recv_sem=block_recv.at[kind, chunk],
            device_id={"blk": (me + 2, me - 2, mate)[kind]},
            device_id_type=MESH,
        )

    def score_copy(kind, c):
        here = pl.ds(pl.multiple_of(c * part, part), part)
        return pltpu.make_async_remote_copy(
            src_ref=scores.at[1 + kind, :, here],
            dst_ref=scores.at[3 + kind, :, here],
            send_sem=score_send.at[kind, c],
            recv_sem=score_recv.at[kind, c],
            device_id={"blk": me + 1 + kind},
            device_id_type=MESH,
        )

    note = pltpu.make_async_remote_copy(
        src_ref=notes.at[1],
        dst_ref=notes.at[0],
        send_sem=note_send,
        recv_sem=note_recv,
        device_id={"blk": me - 1},
        device_id_type=MESH,
    )
    pl.when(has_left)(lambda: note.start())
    bands = height // part
    pieces = part // band_rows

    def outgoing(chunk, act):
        pl.when(has_next)(lambda: act(block_copy(AHEAD, chunk)))
        pl.when(has_prev)(lambda: act(block_copy(BEHIND, chunk)))
        pl.when(odd == 1)(lambda: act(block_copy(BESIDE, chunk)))

    def start_blocks(chunk):
        outgoing(chunk, lambda copy: copy.start())

    def sent_blocks(chunk):
        outgoing(chunk, lambda copy: copy.wait_send())

    for chunk in range(IN_FLIGHT):
        start_blocks(chunk)

    local = [
        pltpu.make_async_copy(src, dst, local_sem.at[i])
        for i, (src, dst) in enumerate(
            (
                (hidden_in, hidden_ref),
                (context_in, context_ref),
                (weights_in, narrow_ref),
                (left_in, left_ref),
                (block_in, right_ref),
                (table_in, table_ref),
                (grad_in, grad_ref),
            )
        )
    ]
    for copy in local:
        copy.start()

    def edges(ref, number, c=None):
        rows = slice(None) if c is None else pl.ds(pl.multiple_of(c * part, part), part)
        sems = (number,) if c is None else (number, c)
        to_left = pltpu.make_async_remote_copy(
            src_ref=ref.at[pl.ds(2, 2), rows],
            dst_ref=ref.at[pl.ds(width + 2, 2), rows],
            send_sem=(send_sem if c is None else rim_send).at[(*sems, 0)],
            recv_sem=(recv_sem if c is None else rim_recv).at[(*sems, 0)],
            device_id={"blk": me - 1},
            device_id_type=MESH,
        )
        to_right = pltpu.make_async_remote_copy(
            src_ref=ref.at[pl.ds(width, 2), rows],
            dst_ref=ref.at[pl.ds(0, 2), rows],
            send_sem=(send_sem if c is None else rim_send).at[(*sems, 1)],
            recv_sem=(recv_sem if c is None else rim_recv).at[(*sems, 1)],
            device_id={"blk": me + 1},
            device_id_type=MESH,
        )
        return to_left, to_right

    def send_edges(ref, number, c=None):
        to_left, to_right = edges(ref, number, c)
        pl.when(has_left)(lambda: to_left.start())
        pl.when(has_right)(lambda: to_right.start())

    def wait_edges(ref, number, c=None):
        to_left, to_right = edges(ref, number, c)
        pl.when(has_left)(lambda: to_left.wait_send())
        pl.when(has_right)(lambda: to_right.wait_send())
        pl.when(has_right)(lambda: to_left.wait_recv())
        pl.when(has_left)(lambda: to_right.wait_recv())

    @pl.when(me < 2)
    def _():
        prior_ref[...] = jnp.zeros(prior_ref.shape, bf16)
        scores[4] = jnp.zeros(scores.shape[1:], bf16)

    @pl.when(me < 1)
    def _():
        scores[3] = jnp.zeros(scores.shape[1:], bf16)

    def prepare(c):
        rows = pl.ds(pl.multiple_of(c * part, part), part)
        x0[pl.ds(2, width), rows, pl.ds(0, hd)] = jnp.swapaxes(
            hidden_ref[rows].astype(f32), 0, 1
        ).astype(bf16)
        for gate in range(3):
            ctx0[gate, :, rows] = jnp.swapaxes(context_ref[gate, rows].astype(f32), 0, 1)

    mixed = narrow_ref.shape[2]
    channel = lax.broadcasted_iota(jnp.int32, (4 * hd, mixed), 0)
    column = lax.broadcasted_iota(jnp.int32, (4 * hd, mixed), 1)
    wanted = jnp.where(channel < 2 * hd, 2 * channel, 2 * channel - 4 * hd + 1)
    inside = lax.rem(channel, 2 * hd) < mixed // 2
    picks[...] = jnp.where((wanted == column) & inside, 1.0, 0.0).astype(bf16)

    def sort_weights(gate):
        @pl.loop(0, taps)
        def _(k):
            sorted_rows = jnp.dot(picks[...], narrow_ref[gate, k], preferred_element_type=f32).astype(bf16)
            weights_ref[0, gate, k] = sorted_rows[: 2 * hd]
            weights_ref[1, gate, k] = sorted_rows[2 * hd :]

    span, lanes = scores.shape[1], scores.shape[3]
    groups = lanes // width

    def score(left, right):
        return jnp.einsum("hxc,hjc->hxj", left, right, preferred_element_type=f32)

    def packed(values):
        parts = [values[:, g * span : (g + 1) * span] for g in range(groups)]
        return jnp.swapaxes(jnp.concatenate(parts, axis=-1), 0, 1).astype(bf16)

    def correlate(c):
        rows = pl.ds(pl.multiple_of(c * part, part), part)
        right, prior, first = right_ref[rows], prior_ref[rows], first_ref[rows]
        close = notes[0, :, pl.ds(0, width)][None] < 1.5
        scores[0, :, rows] = packed(score(left_ref[rows], jnp.where(offset == 0, right, prior)))
        scores[1, :, rows] = packed(jnp.where(close, score(first, right), score(first, prior)))
        scores[2, :, rows] = packed(score(second_ref[rows], prior))

    swapped = (offset == 1) | (offset == 3)

    def pass_on(chunk):
        @pl.when(has_next)
        def _():
            block_copy(BEHIND, chunk).wait_recv()
            pl.when(odd == 0)(lambda: block_copy(BESIDE, chunk, True).start())

        sent_blocks(chunk)
        pl.when(chunk + IN_FLIGHT < BAND_CHUNKS)(lambda: start_blocks(chunk + IN_FLIGHT))

    def meet(c):
        for chunk in [c * pieces + p for p in range(pieces)]:
            pl.when(has_prev)(lambda: block_copy(AHEAD, chunk).wait_recv())
            pl.when(has_right)(lambda: block_copy(BESIDE, chunk).wait_recv())
        correlate(c)
        pl.when(has_right)(lambda: score_copy(0, c).start())
        pl.when(has_next)(lambda: score_copy(1, c).start())

    def features(c):
        pl.when(has_left)(lambda: score_copy(0, c).wait_recv())
        pl.when(has_prev)(lambda: score_copy(1, c).wait_recv())
        rows = pl.ds(pl.multiple_of(c * part, part), part)
        even = jnp.where(offset == 3, scores[4, :, rows], scores[0, :, rows])
        other = scores[3, :, rows]
        low = jnp.where(swapped, even, other)
        high = jnp.where(swapped, other, even)
        window = jnp.concatenate([low, high], axis=-1)
        feats = jnp.einsum("ihj,ijf->ihf", window, table_ref[...], preferred_element_type=f32)
        feats = jnp.concatenate([feats[:, :, g * hd : (g + 1) * hd] for g in range(groups)], axis=0)
        x0[pl.ds(2, width), rows, pl.ds(hd, hd)] = feats.astype(bf16)
        x1[pl.ds(2 + c * part, part), :, pl.ds(hd, hd)] = jnp.swapaxes(feats, 0, 1).astype(bf16)
        send_edges(x0, 0, c)

    def view(section, c):
        if section:
            here = (pl.ds(c * part, part),)
            inner = (pl.ds(c * part + 2, part),)
            return here, inner, lambda k: (pl.ds(c * part + k, part), slice(None))
        rows = pl.ds(pl.multiple_of(c * part, part), part)
        return (slice(None), rows), (pl.ds(2, width), rows), lambda k: (pl.ds(k, width), rows)

    def gates(section, x, rx, z, r, context, c):
        here, inner, at = view(section, c)
        stack = jnp.concatenate([flat(x[at(k)]) for k in range(taps)], axis=1)
        w = jnp.concatenate([flat(weights_ref[section, gate]) for gate in range(2)], axis=1)
        total = jnp.dot(stack, w, preferred_element_type=f32)
        own = x[(*at(2), pl.ds(0, hd))].astype(f32)
        z[here] = jax.nn.sigmoid(total[:, :hd].reshape(own.shape) + context(0, here))
        reset = jax.nn.sigmoid(total[:, hd:].reshape(own.shape) + context(1, here))
        r[here] = reset
        rx[inner] = (reset * own).astype(bf16)

    def gated(x, rx, there):
        return jnp.concatenate([flat(rx[there]), flat(x[(*there, pl.ds(hd, hd))])], axis=1)

    def candidate(section, x, rx, context, c):
        here, _, at = view(section, c)
        stack = jnp.concatenate([gated(x, rx, at(k)) for k in range(taps)], axis=1)
        total = jnp.dot(stack, flat(weights_ref[section, 2]), preferred_element_type=f32)
        near = context(2, here)
        return jnp.tanh(total.reshape(near.shape) + near)

    def context_h(gate, here):
        return ctx0[(gate, *here)]

    def context_v(gate, here):
        return context_ref[(gate, *here)].astype(f32)

    def reset_h(c):
        wait_edges(x0, 0, c)
        gates(0, x0, rx0, z0, r0, context_h, c)
        send_edges(rx0, 1, c)

    def blend_h(c):
        wait_edges(rx0, 1, c)
        here, inner, _ = view(0, c)
        q = candidate(0, x0, rx0, context_h, c)
        q0[here] = q
        z = z0[here]
        own = x0[(*inner, pl.ds(0, hd))].astype(f32)
        blended = (1.0 - z) * own + z * q
        x1[pl.ds(2 + c * part, part), :, pl.ds(0, hd)] = jnp.swapaxes(blended, 0, 1).astype(bf16)

    def arrived(t):
        @pl.when(t == 0)
        def _():
            for copy in local[:5]:
                copy.wait()
            pl.when(has_right)(lambda: note.wait_recv())

        pl.when(t == 1)(lambda: local[5].wait())
        pl.when(t == 2)(lambda: local[6].wait())

    def reset_v(c):
        gates(1, x1, rx1, z1, r1, context_v, c)

    def deltas(g, z, q, own, dq, dzr, inner):
        dq[inner] = (g * z * (1.0 - q * q)).astype(bf16)
        dzr[inner, :, pl.ds(0, hd)] = (g * (q - own) * z * (1.0 - z)).astype(bf16)

    def blend_v(c):
        here = pl.ds(c * part, part)
        inner = pl.ds(c * part + 2, part)
        q = candidate(1, x1, rx1, context_v, c)
        z = z1[here]
        own = x1[inner, :, pl.ds(0, hd)].astype(f32)
        new_ref[here] = ((1.0 - z) * own + z * q).astype(bf16)
        deltas(grad_ref[here], z, q, own, dq1, dzr1, inner)

    @pl.loop(0, bands)
    def _(t):
        pass_on(2 * t)
        arrived(t)
        pl.when(t >= 1)(lambda: meet(t - 1))
        pl.when(t >= 2)(lambda: reset_h(t - 2))
        pl.when(t == 0)(lambda: sort_weights(0))
        pass_on(2 * t + 1)
        prepare(t)
        pl.when(t >= 1)(lambda: features(t - 1))
        pl.when(t >= 2)(lambda: blend_h(t - 2))
        pl.when(t < 2)(lambda: sort_weights(t + 1))

    last = bands - 1
    meet(last)
    reset_h(last - 1)
    reset_v(0)
    features(last)
    blend_h(last - 1)
    reset_v(1)
    reset_h(last)
    blend_v(0)
    blend_h(last)

    @pl.loop(2, height // part)
    def _(c):
        reset_v(c)

    @pl.loop(1, height // part)
    def _(c):
        blend_v(c)

    def back_reset(section, x, g, z, r, dq, dzr, c):
        here = pl.ds(c * part, part)
        inner = pl.ds(c * part + 2, part)
        stack = jnp.concatenate([flat(dq[pl.ds(c * part + taps - 1 - k, part)]) for k in range(taps)], axis=1)
        w = jnp.concatenate([weights_ref[section, 2, k, pl.ds(0, hd)] for k in range(taps)], axis=1)
        total = lax.dot_general(stack, w, NT, preferred_element_type=f32)
        total = total.reshape((part,) + x.shape[1:2] + (hd,))
        reset = r[here]
        own = x[inner, :, pl.ds(0, hd)].astype(f32)
        dzr[inner, :, pl.ds(hd, hd)] = (total * own * reset * (1.0 - reset)).astype(bf16)
        r[here] = g[here] * (1.0 - z[here]) + total * reset

    def back_hidden(section, r, dzr, c):
        stack = jnp.concatenate([flat(dzr[pl.ds(c * part + taps - 1 - k, part)]) for k in range(taps)], axis=1)
        w = jnp.concatenate(
            [weights_ref[section, gate, k, pl.ds(0, hd)] for k in range(taps) for gate in range(2)], axis=1
        )
        total = lax.dot_general(stack, w, NT, preferred_element_type=f32)
        total = total.reshape((part,) + dzr.shape[1:2] + (hd,))
        return r[pl.ds(c * part, part)] + total

    gate_rows = taps * piece
    places, parcels, blanks = layout
    for first, length in blanks:
        g_ref[pl.ds(first, length)] = jnp.zeros((length, hd), f32)

    def weight_grads(section, gates, blocks, d_ref, taken):
        lanes = pl.ds(gates[0] % 2 * hd, len(gates) * hd)
        rows = pl.ds(0, len(gates) * hd)
        acc[:, rows] = jnp.zeros((taps, len(gates) * hd, 2 * hd), f32)

        @pl.loop(0, blocks)
        def _(c):
            d = flat(d_ref[pl.ds(c * part + 2, part), :, lanes]).astype(f32).T.astype(bf16)
            for k in range(taps):
                acc[k, rows] += jnp.dot(d, taken(c * part + k), preferred_element_type=f32)

        for k in range(taps):
            for at, gate in enumerate(gates):
                place = places[section, gate] + k * piece
                g_ref[pl.ds(place, piece)] = acc[k, pl.ds(at * hd, hd)].T[:piece]

    def plain(x):
        return lambda first: flat(x[pl.ds(first, part)])

    spans = []
    landing = []
    for order, (base, total_rows) in zip(orders, parcels):
        row = [(base, total_rows)]
        places_in = [base]
        for group in order:
            first, length = row[-1]
            share = length // size(group)
            row.append((pl.multiple_of(first + rank(group) * share, 16), share))
            places_in.append(places_in[-1] + length - share)
        spans.append(row)
        landing.append(places_in)

    def away(section, step, d):
        group = orders[section][step]
        target, scale = 0, 1
        for at in group:
            axis, stride, members = steps[at]
            there = dict(split(group, d)).get(at, 0)
            place = partner(((at, there),))[axis]
            target = target + lax.rem(place // stride, members) * scale
            scale *= members
        share = spans[section][step + 1][1]
        return pl.ds(pl.multiple_of(spans[section][step][0] + target * share, 16), share)

    def stage_of(section, k):
        depth = len(orders[section])
        step = k if k < depth else 2 * depth - 1 - k
        return depth, step, orders[section][step]

    def begin(section, k):
        depth, step, group = stage_of(section, k)
        own, share = spans[section][step + 1]
        for d in range(1, size(group)):
            if k < depth:
                there = away(section, step, d)
                sbuf[there] = g_ref[there].astype(bf16)
                src = sbuf.at[there]
                dst = rbuf.at[pl.ds(landing[section][step] + (d - 1) * share, share)]
            else:
                src = dst = sum_ref.at[pl.ds(own, share)]
            pltpu.make_async_remote_copy(
                src_ref=src,
                dst_ref=dst,
                send_sem=sum_send.at[section, k],
                recv_sem=sum_recv.at[section, k],
                device_id=partner(split(group, d)),
                device_id_type=MESH,
            ).start()

    def grad_copy(section):
        first, length = parcels[section]
        whole = pl.ds(first, length)
        return pltpu.make_async_copy(sum_ref.at[whole], grads_out.at[whole], out_sem.at[2 + section])

    def finish(section, k):
        depth, step, group = stage_of(section, k)
        keep, share = spans[section][step + 1]
        moved = pl.ds(landing[section][step if k < depth else 0], (size(group) - 1) * share)
        for sem in (sum_send, sum_recv):
            ref = rbuf if k < depth else sum_ref
            pltpu.make_async_copy(ref.at[moved], ref.at[moved], sem.at[section, k]).wait()
        if k < depth:
            here = pl.ds(keep, share)
            summed = g_ref[here]
            for d in range(1, size(group)):
                landed = rbuf[pl.ds(landing[section][step] + (d - 1) * share, share)]
                summed = summed + landed.astype(f32)
            if k == depth - 1:
                sum_ref[here] = summed.astype(bf16)
            else:
                g_ref[here] = summed
        elif k == 2 * depth - 1:
            grad_copy(section).start()

    def turn(section, k):
        last = 2 * len(orders[section]) - 1
        if 0 <= k <= last:
            finish(section, k)
        if k < last:
            begin(section, k + 1)

    new_copy = pltpu.make_async_copy(new_ref, new_out, out_sem.at[0])
    new_copy.start()

    @pl.loop(0, height // part)
    def _(c):
        back_reset(1, x1, grad_ref, z1, r1, dq1, dzr1, c)

    blocks_h, blocks_v = width // part, height // part
    weight_grads(1, (0, 1), blocks_v, dzr1, plain(x1))
    weight_grads(1, (2,), blocks_v, dq1, lambda first: gated(x1, rx1, (pl.ds(first, part), slice(None))))
    turn(0, -1)

    @pl.loop(0, height // part)
    def _(c):
        rows = pl.ds(pl.multiple_of(c * part, part), part)
        g0[:, rows] = jnp.swapaxes(back_hidden(1, r1, dzr1, c), 0, 1)

    @pl.loop(0, width // part)
    def _(c):
        here = pl.ds(c * part, part)
        inner = pl.ds(c * part + 2, part)
        own = x0[inner, :, pl.ds(0, hd)].astype(f32)
        deltas(g0[here], z0[here], q0[here], own, dq0, dzr0, inner)

    send_edges(dq0, 0)
    turn(0, 0)
    weight_grads(0, (2,), blocks_h, dq0, lambda first: gated(x0, rx0, (pl.ds(first, part), slice(None))))
    weight_grads(0, (0,), blocks_h, dzr0, plain(x0))
    turn(1, -1)
    wait_edges(dq0, 0)

    @pl.loop(0, width // part)
    def _(c):
        back_reset(0, x0, g0, z0, r0, dq0, dzr0, c)

    send_edges(dzr0, 1)
    turn(0, 1)
    turn(1, 0)
    weight_grads(0, (1,), blocks_h, dzr0, plain(x0))
    turn(2, -1)
    wait_edges(dzr0, 1)

    @pl.loop(0, width // part)
    def _(c):
        cols = pl.ds(pl.multiple_of(c * part, part), part)
        hidden_back_ref[:, cols] = jnp.swapaxes(back_hidden(0, r0, dzr0, c), 0, 1)

    back_copy = pltpu.make_async_copy(hidden_back_ref, hidden_back_out, out_sem.at[1])
    back_copy.start()

    for k in range(2 * len(steps)):
        turn(2, k)
        turn(0, k + 2)
        turn(1, k + 1)

    new_copy.wait()
    back_copy.wait()
    for section in range(len(parcels)):
        grad_copy(section).wait()
    pl.when(has_left)(lambda: note.wait_send())
    for c in range(BAND_CHUNKS):
        pl.when((odd == 0) & has_next)(lambda c=c: block_copy(BESIDE, c, True).wait_send())
    for c in range(bands):
        pl.when(has_right)(lambda c=c: score_copy(0, c).wait_send())
        pl.when(has_next)(lambda c=c: score_copy(1, c).wait_send())


def finish_kernel(
    places, new_in, back_in, sums_in, new_out, back_out, grads_out, new, back, sums, rows, grads, sems
):
    sections, gates = 2, len(places) // 2
    taps, mixed = grads.shape[1:3]
    depth = mixed // sections
    piece = -(-depth // 8) * 8
    load = pltpu.make_async_copy(sums_in, sums, sems.at[0])
    load.start()
    enter = [pltpu.make_async_copy(new_in, new, sems.at[1]), pltpu.make_async_copy(back_in, back, sems.at[2])]
    for copy in enter:
        copy.start()
    load.wait()
    through = []
    for gate in range(gates):
        for section in range(sections):
            first = places[section, gate]
            there = pl.ds(first // 16 * 16, -(-(first + taps * piece) // 16) * 16 - first // 16 * 16)
            rows[there] = sums[there].astype(jnp.float32)
            for tap in range(taps):
                taken = rows[pl.ds(first + tap * piece, depth)]
                grads[gate, tap, pl.ds(section, depth, stride=sections)] = taken
        through.append(pltpu.make_async_copy(grads.at[gate], grads_out.at[gate], sems.at[3 + gate]))
        through[-1].start()
        if gate == 0:
            for copy in enter:
                copy.wait()
            for at, (held, out) in enumerate(((new, new_out), (back, back_out))):
                through.append(pltpu.make_async_copy(held, out, sems.at[1 + at]))
                through[-1].start()
    for copy in through:
        copy.wait()


def finished(new_hidden, hidden_back, sums, places, shape):
    anywhere = pl.BlockSpec(memory_space=pl.ANY)
    f32 = jnp.float32
    return pl.pallas_call(
        functools.partial(finish_kernel, places),
        out_shape=(
            jax.ShapeDtypeStruct(new_hidden.shape, new_hidden.dtype),
            jax.ShapeDtypeStruct(hidden_back.shape, hidden_back.dtype),
            jax.ShapeDtypeStruct(shape, f32),
        ),
        in_specs=[anywhere] * 3,
        out_specs=(anywhere,) * 3,
        scratch_shapes=[
            pltpu.VMEM(new_hidden.shape, new_hidden.dtype),
            pltpu.VMEM(hidden_back.shape, hidden_back.dtype),
            pltpu.VMEM(sums.shape, sums.dtype),
            pltpu.VMEM(sums.shape, f32),
            pltpu.VMEM(shape, f32),
            pltpu.SemaphoreType.DMA((3 + shape[0],)),
        ],
        compiler_params=pltpu.CompilerParams(vmem_limit_bytes=58 * 1024 * 1024),
        name="finish",
    )(new_hidden, hidden_back, sums)


def core(offset, block, left, table, hidden, context, weights, hidden_grad, pairs, count, piece):
    height, width, hd = hidden.shape
    taps = weights.shape[1]
    bf16, f32 = jnp.bfloat16, jnp.float32
    anywhere = pl.BlockSpec(memory_space=pl.ANY)
    steps = sum_steps(pairs, count)
    lanes = hd
    gate_rows = taps * piece
    layout = sum_layout(gate_rows, pairs * count)
    sum_rows = sum(length for _, length in layout[1])

    def held(values):
        return pltpu.VMEM(values.shape, values.dtype)

    across = (width, height, hd)
    down = (height, width, hd)

    def padded(shape, wide):
        return pltpu.VMEM((shape[0] + 4, shape[1], wide * hd), bf16)

    return pl.pallas_call(
        functools.partial(core_kernel, count, piece, steps, layout),
        out_shape=(
            jax.ShapeDtypeStruct(hidden.shape, bf16),
            jax.ShapeDtypeStruct(hidden.shape, f32),
            jax.ShapeDtypeStruct((sum_rows, hd), bf16),
        ),
        in_specs=[pl.BlockSpec(memory_space=pltpu.SMEM)] + [anywhere] * 7,
        out_specs=(anywhere,) * 3,
        scratch_shapes=[
            held(hidden),
            pltpu.VMEM(hidden.shape, f32),
            pltpu.VMEM((sum_rows, hd), bf16),
            held(block),
            held(block),
            held(left),
            held(left),
            held(left),
            pltpu.VMEM((5, width * width // lanes, height, lanes), bf16),
            pltpu.VMEM((2, width, lanes), f32),
            held(table),
            held(hidden),
            held(context),
            held(weights),
            pltpu.VMEM((4 * hd, weights.shape[2]), bf16),
            held(hidden_grad),
            pltpu.VMEM((2, 3, taps, 2 * hd, hd), bf16),
            pltpu.VMEM((sum_rows, hd), f32),
            pltpu.VMEM((sum_rows, hd), bf16),
            pltpu.VMEM((sum_rows, hd), bf16),
            padded(across, 2),
            padded(down, 2),
            padded(across, 1),
            padded(down, 1),
            padded(across, 1),
            padded(down, 1),
            padded(across, 2),
            padded(down, 2),
            pltpu.VMEM((3,) + across, f32),
            pltpu.VMEM(across, f32),
            pltpu.VMEM(across, f32),
            pltpu.VMEM(across, f32),
            pltpu.VMEM(down, f32),
            pltpu.VMEM(down, f32),
            pltpu.VMEM(across, f32),
            pltpu.VMEM((taps, 2 * hd, 2 * hd), f32),
            pltpu.SemaphoreType.DMA((2, 2)),
            pltpu.SemaphoreType.DMA((2, 2)),
            pltpu.SemaphoreType.DMA((3, BAND_CHUNKS)),
            pltpu.SemaphoreType.DMA((3, BAND_CHUNKS)),
            pltpu.SemaphoreType.DMA((2, height // 16)),
            pltpu.SemaphoreType.DMA((2, height // 16)),
            pltpu.SemaphoreType.DMA(()),
            pltpu.SemaphoreType.DMA(()),
            pltpu.SemaphoreType.DMA((2, height // 16, 2)),
            pltpu.SemaphoreType.DMA((2, height // 16, 2)),
            pltpu.SemaphoreType.DMA((3, 2 * len(steps))),
            pltpu.SemaphoreType.DMA((3, 2 * len(steps))),
            pltpu.SemaphoreType.DMA((7,)),
            pltpu.SemaphoreType.DMA((5,)),
        ],
        compiler_params=pltpu.CompilerParams(
            collective_id=0, has_side_effects=True, vmem_limit_bytes=58 * 1024 * 1024
        ),
        name="core",
    )(offset, block, left, table, hidden, context, weights, hidden_grad)


def on_device(left_feats, right_feats, offsets, hidden, context, gru_weights, hidden_grad):
    left_block = left_feats[0]
    right_block = right_feats[0]
    column_count = left_block.shape[1]
    table = lookup_table(column_count, LEVELS, RADIUS) / math.sqrt(left_block.shape[-1])
    hd = gru_weights.shape[-1]
    table = packed_table(table, hd)
    table = jnp.asarray(table, jnp.bfloat16)
    pairs, blks = lax.axis_size("pair"), lax.axis_size("blk")
    shape = gru_weights.shape
    piece = -(-shape[3] // 8) * 8
    gate_rows = shape[2] * piece
    mixed = shape[1:3] + (shape[0] * shape[3], hd)
    new_hidden, hidden_back, sums = core(
        offsets,
        right_block,
        left_block,
        table,
        hidden[0],
        context[0],
        jnp.transpose(gru_weights, (1, 2, 3, 0, 4)).reshape(mixed),
        hidden_grad[0],
        pairs,
        blks,
        piece,
    )
    places = sum_layout(gate_rows, pairs * blks)[0]
    new_hidden, hidden_back, grads = finished(new_hidden, hidden_back, sums, places, mixed)
    grads = grads.reshape(shape[1:4] + (shape[0], hd))
    return (new_hidden[None], jnp.transpose(grads, (3, 0, 1, 2, 4)), hidden_back[None])


def solution(mesh):
    placed = (
        P("pair", None, "blk", None),
        P("pair", None, "blk", None),
        P("blk"),
        P("pair", None, "blk", None),
        P("pair", None, None, "blk", None),
        P(),
        P("pair", None, "blk", None),
    )
    return jax.shard_map(
        on_device,
        mesh=mesh,
        in_specs=placed,
        out_specs=(P("pair", None, "blk", None), P(), P("pair", None, "blk", None)),
        check_vma=False,
    )
```

```python
import functools
import math

import jax
import jax.numpy as jnp
import numpy as np
from jax import lax
from jax.experimental import pallas as pl
from jax.experimental.pallas import tpu as pltpu
from jax.sharding import PartitionSpec as P

LEVELS = 4
RADIUS = 4


def lookup_table(column_count, level_count, radius_len):
    tap_count = 2 * radius_len + 1
    lookup = np.zeros((column_count, 2 * column_count, level_count * tap_count), np.float32)
    positions = np.arange(column_count)
    for level_id in range(level_count):
        pool_span = 2**level_id
        pooled_cols = 2 * column_count // pool_span
        for tap_id in range(tap_count):
            centre = (positions + column_count // 2) // pool_span + tap_id - radius_len
            inside = (centre >= 0) & (centre < pooled_cols)
            for inner_id in range(pool_span):
                lookup[
                    positions[inside],
                    centre[inside] * pool_span + inner_id,
                    level_id * tap_count + tap_id,
                ] = (
                    1.0 / pool_span
                )
    return lookup


def packed_table(lookup, lanes):
    width, _, feats = lookup.shape
    groups = lanes // width
    span = width // groups
    table = np.zeros((span, 2, groups, width, groups, lanes), np.float32)
    for group in range(groups):
        columns = lookup[group * span : (group + 1) * span].reshape(span, 2, width, feats)
        table[:, :, group, :, group, :feats] = columns
    return table.reshape(span, 2 * lanes, groups * lanes)


MESH = pl.DeviceIdType.MESH
BAND_CHUNKS = 8
IN_FLIGHT = 2


def sum_steps(pairs, blks):
    steps = []
    for axis, size, most in (("pair", pairs, 2), ("blk", blks, 8)):
        stride = 1
        while stride < size:
            members = min(most, size // stride)
            steps.append((axis, stride, members))
            stride *= members
    return steps


def sum_orders(depth):
    along = [(at,) for at in range(depth)]
    return along, along, along


def sum_layout(gate_rows, devices):
    step = devices * 16
    whole = -(-3 * gate_rows // step) * step
    places = {(1, gate): gate * gate_rows for gate in range(3)}
    ready = 2 * gate_rows // step * step
    if ready:
        late = whole + 2 * gate_rows
    else:
        ready = -(-2 * gate_rows // step) * step
        late = whole + ready
    places.update({(0, 2): whole, (0, 0): whole + gate_rows, (0, 1): late})
    rest = -(-(late + gate_rows - whole - ready) // step) * step
    parcels = ((0, whole), (whole, ready), (whole + ready, rest))
    blanks = []
    at = 0
    for first in sorted(places.values()) + [whole + ready + rest]:
        if first > at:
            blanks.append((at, first - at))
        at = first + gate_rows
    return places, parcels, blanks


NT = (((1,), (1,)), ((), ()))


def flat(values):
    return values.reshape(-1, values.shape[-1])


def core_kernel(
    count,
    piece,
    steps,
    layout,
    offset_ref,
    block_in,
    left_in,
    table_in,
    hidden_in,
    context_in,
    weights_in,
    grad_in,
    new_out,
    hidden_back_out,
    grads_out,
    new_ref,
    hidden_back_ref,
    sum_ref,
    right_ref,
    prior_ref,
    left_ref,
    first_ref,
    second_ref,
    scores,
    notes,
    table_ref,
    hidden_ref,
    context_ref,
    narrow_ref,
    picks,
    grad_ref,
    weights_ref,
    g_ref,
    sbuf,
    rbuf,
    x0,
    x1,
    rx0,
    rx1,
    dq0,
    dq1,
    dzr0,
    dzr1,
    ctx0,
    z0,
    r0,
    q0,
    z1,
    r1,
    g0,
    acc,
    send_sem,
    recv_sem,
    block_send,
    block_recv,
    score_send,
    score_recv,
    note_send,
    note_recv,
    rim_send,
    rim_recv,
    sum_send,
    sum_recv,
    local_sem,
    out_sem,
):
    height, width, hd = hidden_ref.shape
    taps = weights_ref.shape[2]
    me = lax.axis_index("blk")
    has_left = me >= 1
    has_right = me + 1 < count
    bf16, f32 = jnp.bfloat16, jnp.float32
    part = 16

    for ref in (x0, x1, rx0, rx1, dq0, dq1, dzr0, dzr1):
        edge = jnp.zeros((2,) + ref.shape[1:], bf16)
        ref[pl.ds(0, 2)] = edge
        ref[pl.ds(ref.shape[0] - 2, 2)] = edge

    offset = offset_ref[0]
    notes[1] = jnp.full(notes.shape[1:], offset, jnp.int32).astype(f32)

    barrier = pltpu.get_barrier_semaphore()
    position = {"pair": lax.axis_index("pair"), "blk": me}
    orders = sum_orders(len(steps))
    digits = [lax.rem(position[axis] // stride, members) for axis, stride, members in steps]

    def partner(apart):
        places = {}
        for at, d in apart:
            axis, stride, members = steps[at]
            place = places.get(axis, position[axis])
            mask = 1
            while mask < members:
                if d & mask:
                    bit = lax.rem(digits[at] // mask, 2)
                    place = place + stride * mask * (1 - 2 * bit)
                mask *= 2
            places[axis] = place
        return places

    def split(group, d):
        apart = []
        for at in group:
            members = steps[at][2]
            if d % members:
                apart.append((at, d % members))
            d //= members
        return tuple(apart)

    def size(group):
        return math.prod(steps[at][2] for at in group)

    def rank(group):
        total, scale = 0, 1
        for at in group:
            total = total + digits[at] * scale
            scale *= steps[at][2]
        return total

    met = sorted({split(group, d) for order in orders for group in order for d in range(1, size(group))})
    for apart in met:
        pl.semaphore_signal(barrier, inc=1, device_id=partner(apart), device_id_type=MESH)
    has_next = me + 2 < count
    has_prev = me >= 2
    expected = len(met)
    for present, shift in ((has_left, -1), (has_right, 1), (has_prev, -2), (has_next, 2)):

        @pl.when(present)
        def _(shift=shift):
            pl.semaphore_signal(barrier, inc=1, device_id={"blk": me + shift}, device_id_type=MESH)

        expected = expected + present.astype(jnp.int32)
    pl.semaphore_wait(barrier, expected)

    odd = lax.rem(me, 2)
    mate = me + 1 - 2 * odd
    band_rows = height // BAND_CHUNKS

    AHEAD, BEHIND, BESIDE = range(3)

    def block_copy(kind, chunk, relay=False):
        here = pl.ds(chunk * band_rows, band_rows)
        src = (block_in, left_in, second_ref if relay else left_in)[kind]
        dst = (prior_ref, second_ref, first_ref)[kind]
        return pltpu.make_async_remote_copy(
            src_ref=src.at[here],
            dst_ref=dst.at[here],
            send_sem=block_send.at[kind, chunk],
            recv_sem=block_recv.at[kind, chunk],
            device_id={"blk": (me + 2, me - 2, mate)[kind]},
            device_id_type=MESH,
        )

    def score_copy(kind, c):
        return pltpu.make_async_remote_copy(
            src_ref=scores.at[1 + kind, c],
            dst_ref=scores.at[3 + kind, c],
            send_sem=score_send.at[kind, c],
            recv_sem=score_recv.at[kind, c],
            device_id={"blk": me + 1 + kind},
            device_id_type=MESH,
        )

    note = pltpu.make_async_remote_copy(
        src_ref=notes.at[1],
        dst_ref=notes.at[0],
        send_sem=note_send,
        recv_sem=note_recv,
        device_id={"blk": me - 1},
        device_id_type=MESH,
    )
    pl.when(has_left)(lambda: note.start())
    bands = height // part
    pieces = part // band_rows

    def outgoing(chunk, act):
        pl.when(has_next)(lambda: act(block_copy(AHEAD, chunk)))
        pl.when(has_prev)(lambda: act(block_copy(BEHIND, chunk)))
        pl.when(odd == 1)(lambda: act(block_copy(BESIDE, chunk)))

    def start_blocks(chunk):
        outgoing(chunk, lambda copy: copy.start())

    def sent_blocks(chunk):
        outgoing(chunk, lambda copy: copy.wait_send())

    for chunk in range(IN_FLIGHT):
        start_blocks(chunk)

    local = [
        pltpu.make_async_copy(src, dst, local_sem.at[i])
        for i, (src, dst) in enumerate(
            (
                (hidden_in, hidden_ref),
                (context_in, context_ref),
                (weights_in, narrow_ref),
                (left_in, left_ref),
                (block_in, right_ref),
                (table_in, table_ref),
                (grad_in, grad_ref),
            )
        )
    ]
    for copy in local:
        copy.start()

    def edges(ref, number, c=None):
        rows = slice(None) if c is None else pl.ds(pl.multiple_of(c * part, part), part)
        sems = (number,) if c is None else (number, c)
        to_left = pltpu.make_async_remote_copy(
            src_ref=ref.at[pl.ds(2, 2), rows],
            dst_ref=ref.at[pl.ds(width + 2, 2), rows],
            send_sem=(send_sem if c is None else rim_send).at[(*sems, 0)],
            recv_sem=(recv_sem if c is None else rim_recv).at[(*sems, 0)],
            device_id={"blk": me - 1},
            device_id_type=MESH,
        )
        to_right = pltpu.make_async_remote_copy(
            src_ref=ref.at[pl.ds(width, 2), rows],
            dst_ref=ref.at[pl.ds(0, 2), rows],
            send_sem=(send_sem if c is None else rim_send).at[(*sems, 1)],
            recv_sem=(recv_sem if c is None else rim_recv).at[(*sems, 1)],
            device_id={"blk": me + 1},
            device_id_type=MESH,
        )
        return to_left, to_right

    def send_edges(ref, number, c=None):
        to_left, to_right = edges(ref, number, c)
        pl.when(has_left)(lambda: to_left.start())
        pl.when(has_right)(lambda: to_right.start())

    def wait_edges(ref, number, c=None):
        to_left, to_right = edges(ref, number, c)
        pl.when(has_left)(lambda: to_left.wait_send())
        pl.when(has_right)(lambda: to_right.wait_send())
        pl.when(has_right)(lambda: to_left.wait_recv())
        pl.when(has_left)(lambda: to_right.wait_recv())

    @pl.when(me < 2)
    def _():
        prior_ref[...] = jnp.zeros(prior_ref.shape, bf16)
        scores[4] = jnp.zeros(scores.shape[1:], bf16)

    @pl.when(me < 1)
    def _():
        scores[3] = jnp.zeros(scores.shape[1:], bf16)

    def prepare(c):
        rows = pl.ds(pl.multiple_of(c * part, part), part)
        x0[pl.ds(2, width), rows, pl.ds(0, hd)] = jnp.swapaxes(
            hidden_ref[rows].astype(f32), 0, 1
        ).astype(bf16)
        for gate in range(3):
            ctx0[gate, :, rows] = jnp.swapaxes(context_ref[gate, rows].astype(f32), 0, 1)

    mixed = narrow_ref.shape[2]
    channel = lax.broadcasted_iota(jnp.int32, (4 * hd, mixed), 0)
    column = lax.broadcasted_iota(jnp.int32, (4 * hd, mixed), 1)
    wanted = jnp.where(channel < 2 * hd, 2 * channel, 2 * channel - 4 * hd + 1)
    inside = lax.rem(channel, 2 * hd) < mixed // 2
    picks[...] = jnp.where((wanted == column) & inside, 1.0, 0.0).astype(bf16)

    def sort_weights(gate):
        @pl.loop(0, taps)
        def _(k):
            sorted_rows = jnp.dot(picks[...], narrow_ref[gate, k], preferred_element_type=f32).astype(bf16)
            weights_ref[0, gate, k] = sorted_rows[: 2 * hd]
            weights_ref[1, gate, k] = sorted_rows[2 * hd :]

    span, lanes = scores.shape[2], scores.shape[4]
    groups = lanes // width

    def score(left, right):
        return jnp.einsum("hxc,hjc->hxj", left, right, preferred_element_type=f32)

    def packed(values):
        parts = [values[:, g * span : (g + 1) * span] for g in range(groups)]
        return jnp.swapaxes(jnp.concatenate(parts, axis=-1), 0, 1).astype(bf16)

    def correlate(c):
        rows = pl.ds(pl.multiple_of(c * part, part), part)
        right, prior, first = right_ref[rows], prior_ref[rows], first_ref[rows]
        close = notes[0, :, pl.ds(0, width)][None] < 1.5
        scores[0, c] = packed(score(left_ref[rows], jnp.where(offset == 0, right, prior)))
        scores[1, c] = packed(jnp.where(close, score(first, right), score(first, prior)))
        scores[2, c] = packed(score(second_ref[rows], prior))

    swapped = (offset == 1) | (offset == 3)

    def pass_on(chunk):
        @pl.when(has_next)
        def _():
            block_copy(BEHIND, chunk).wait_recv()
            pl.when(odd == 0)(lambda: block_copy(BESIDE, chunk, True).start())

        sent_blocks(chunk)
        pl.when(chunk + IN_FLIGHT < BAND_CHUNKS)(lambda: start_blocks(chunk + IN_FLIGHT))

    def meet(c):
        for chunk in [c * pieces + p for p in range(pieces)]:
            pl.when(has_prev)(lambda: block_copy(AHEAD, chunk).wait_recv())
            pl.when(has_right)(lambda: block_copy(BESIDE, chunk).wait_recv())
        correlate(c)
        pl.when(has_right)(lambda: score_copy(0, c).start())
        pl.when(has_next)(lambda: score_copy(1, c).start())

    def features(c):
        pl.when(has_left)(lambda: score_copy(0, c).wait_recv())
        pl.when(has_prev)(lambda: score_copy(1, c).wait_recv())
        rows = pl.ds(pl.multiple_of(c * part, part), part)
        even = jnp.where(offset == 3, scores[4, c], scores[0, c])
        other = scores[3, c]
        low = jnp.where(swapped, even, other)
        high = jnp.where(swapped, other, even)
        window = jnp.concatenate([low, high], axis=-1)
        feats = jnp.einsum("ihj,ijf->ihf", window, table_ref[...], preferred_element_type=f32)
        feats = jnp.concatenate([feats[:, :, g * hd : (g + 1) * hd] for g in range(groups)], axis=0)
        x0[pl.ds(2, width), rows, pl.ds(hd, hd)] = feats.astype(bf16)
        x1[pl.ds(2 + c * part, part), :, pl.ds(hd, hd)] = jnp.swapaxes(feats, 0, 1).astype(bf16)
        send_edges(x0, 0, c)

    def view(section, c):
        if section:
            here = (pl.ds(c * part, part),)
            inner = (pl.ds(c * part + 2, part),)
            return here, inner, lambda k: (pl.ds(c * part + k, part), slice(None))
        rows = pl.ds(pl.multiple_of(c * part, part), part)
        return (slice(None), rows), (pl.ds(2, width), rows), lambda k: (pl.ds(k, width), rows)

    def gates(section, x, rx, z, r, context, c):
        here, inner, at = view(section, c)
        stack = jnp.concatenate([flat(x[at(k)]) for k in range(taps)], axis=1)
        w = jnp.concatenate([flat(weights_ref[section, gate]) for gate in range(2)], axis=1)
        total = jnp.dot(stack, w, preferred_element_type=f32)
        own = x[(*at(2), pl.ds(0, hd))].astype(f32)
        z[here] = jax.nn.sigmoid(total[:, :hd].reshape(own.shape) + context(0, here))
        reset = jax.nn.sigmoid(total[:, hd:].reshape(own.shape) + context(1, here))
        r[here] = reset
        rx[inner] = (reset * own).astype(bf16)

    def gated(x, rx, there):
        return jnp.concatenate([flat(rx[there]), flat(x[(*there, pl.ds(hd, hd))])], axis=1)

    def candidate(section, x, rx, context, c):
        here, _, at = view(section, c)
        stack = jnp.concatenate([gated(x, rx, at(k)) for k in range(taps)], axis=1)
        total = jnp.dot(stack, flat(weights_ref[section, 2]), preferred_element_type=f32)
        near = context(2, here)
        return jnp.tanh(total.reshape(near.shape) + near)

    def context_h(gate, here):
        return ctx0[(gate, *here)]

    def context_v(gate, here):
        return context_ref[(gate, *here)].astype(f32)

    def reset_h(c):
        wait_edges(x0, 0, c)
        gates(0, x0, rx0, z0, r0, context_h, c)
        send_edges(rx0, 1, c)

    def blend_h(c):
        wait_edges(rx0, 1, c)
        here, inner, _ = view(0, c)
        q = candidate(0, x0, rx0, context_h, c)
        q0[here] = q
        z = z0[here]
        own = x0[(*inner, pl.ds(0, hd))].astype(f32)
        blended = (1.0 - z) * own + z * q
        x1[pl.ds(2 + c * part, part), :, pl.ds(0, hd)] = jnp.swapaxes(blended, 0, 1).astype(bf16)

    def arrived(t):
        @pl.when(t == 0)
        def _():
            for copy in local[:5]:
                copy.wait()
            pl.when(has_right)(lambda: note.wait_recv())

        pl.when(t == 1)(lambda: local[5].wait())
        pl.when(t == 2)(lambda: local[6].wait())

    def reset_v(c):
        gates(1, x1, rx1, z1, r1, context_v, c)

    def deltas(g, z, q, own, dq, dzr, inner):
        dq[inner] = (g * z * (1.0 - q * q)).astype(bf16)
        dzr[inner, :, pl.ds(0, hd)] = (g * (q - own) * z * (1.0 - z)).astype(bf16)

    def blend_v(c):
        here = pl.ds(c * part, part)
        inner = pl.ds(c * part + 2, part)
        q = candidate(1, x1, rx1, context_v, c)
        z = z1[here]
        own = x1[inner, :, pl.ds(0, hd)].astype(f32)
        new_ref[here] = ((1.0 - z) * own + z * q).astype(bf16)
        deltas(grad_ref[here], z, q, own, dq1, dzr1, inner)

    @pl.loop(0, bands)
    def _(t):
        pass_on(2 * t)
        arrived(t)
        pl.when(t >= 1)(lambda: meet(t - 1))
        pl.when(t >= 2)(lambda: reset_h(t - 2))
        pl.when(t == 0)(lambda: sort_weights(0))
        pass_on(2 * t + 1)
        prepare(t)
        pl.when(t >= 1)(lambda: features(t - 1))
        pl.when(t >= 2)(lambda: blend_h(t - 2))
        pl.when(t < 2)(lambda: sort_weights(t + 1))

    last = bands - 1
    meet(last)
    reset_h(last - 1)
    reset_v(0)
    features(last)
    blend_h(last - 1)
    reset_v(1)
    reset_h(last)
    blend_v(0)
    blend_h(last)

    @pl.loop(2, height // part)
    def _(c):
        reset_v(c)

    @pl.loop(1, height // part)
    def _(c):
        blend_v(c)

    def back_reset(section, x, g, z, r, dq, dzr, c):
        here = pl.ds(c * part, part)
        inner = pl.ds(c * part + 2, part)
        stack = jnp.concatenate([flat(dq[pl.ds(c * part + taps - 1 - k, part)]) for k in range(taps)], axis=1)
        w = jnp.concatenate([weights_ref[section, 2, k, pl.ds(0, hd)] for k in range(taps)], axis=1)
        total = lax.dot_general(stack, w, NT, preferred_element_type=f32)
        total = total.reshape((part,) + x.shape[1:2] + (hd,))
        reset = r[here]
        own = x[inner, :, pl.ds(0, hd)].astype(f32)
        dzr[inner, :, pl.ds(hd, hd)] = (total * own * reset * (1.0 - reset)).astype(bf16)
        r[here] = g[here] * (1.0 - z[here]) + total * reset

    def back_hidden(section, r, dzr, c):
        stack = jnp.concatenate([flat(dzr[pl.ds(c * part + taps - 1 - k, part)]) for k in range(taps)], axis=1)
        w = jnp.concatenate(
            [weights_ref[section, gate, k, pl.ds(0, hd)] for k in range(taps) for gate in range(2)], axis=1
        )
        total = lax.dot_general(stack, w, NT, preferred_element_type=f32)
        total = total.reshape((part,) + dzr.shape[1:2] + (hd,))
        return r[pl.ds(c * part, part)] + total

    gate_rows = taps * piece
    places, parcels, blanks = layout
    for first, length in blanks:
        g_ref[pl.ds(first, length)] = jnp.zeros((length, hd), f32)

    def weight_grads(section, gates, blocks, d_ref, taken):
        lanes = pl.ds(gates[0] % 2 * hd, len(gates) * hd)
        rows = pl.ds(0, len(gates) * hd)
        acc[:, rows] = jnp.zeros((taps, len(gates) * hd, 2 * hd), f32)

        @pl.loop(0, blocks)
        def _(c):
            d = flat(d_ref[pl.ds(c * part + 2, part), :, lanes]).astype(f32).T.astype(bf16)
            for k in range(taps):
                acc[k, rows] += jnp.dot(d, taken(c * part + k), preferred_element_type=f32)

        for k in range(taps):
            for at, gate in enumerate(gates):
                place = places[section, gate] + k * piece
                g_ref[pl.ds(place, piece)] = acc[k, pl.ds(at * hd, hd)].T[:piece]

    def plain(x):
        return lambda first: flat(x[pl.ds(first, part)])

    spans = []
    landing = []
    for order, (base, total_rows) in zip(orders, parcels):
        row = [(base, total_rows)]
        places_in = [base]
        for group in order:
            first, length = row[-1]
            share = length // size(group)
            row.append((pl.multiple_of(first + rank(group) * share, 16), share))
            places_in.append(places_in[-1] + length - share)
        spans.append(row)
        landing.append(places_in)

    def away(section, step, d):
        group = orders[section][step]
        target, scale = 0, 1
        for at in group:
            axis, stride, members = steps[at]
            there = dict(split(group, d)).get(at, 0)
            place = partner(((at, there),))[axis]
            target = target + lax.rem(place // stride, members) * scale
            scale *= members
        share = spans[section][step + 1][1]
        return pl.ds(pl.multiple_of(spans[section][step][0] + target * share, 16), share)

    def stage_of(section, k):
        depth = len(orders[section])
        step = k if k < depth else 2 * depth - 1 - k
        return depth, step, orders[section][step]

    def begin(section, k):
        depth, step, group = stage_of(section, k)
        own, share = spans[section][step + 1]
        for d in range(1, size(group)):
            if k < depth:
                there = away(section, step, d)
                sbuf[there] = g_ref[there].astype(bf16)
                src = sbuf.at[there]
                dst = rbuf.at[pl.ds(landing[section][step] + (d - 1) * share, share)]
            else:
                src = dst = sum_ref.at[pl.ds(own, share)]
            pltpu.make_async_remote_copy(
                src_ref=src,
                dst_ref=dst,
                send_sem=sum_send.at[section, k],
                recv_sem=sum_recv.at[section, k],
                device_id=partner(split(group, d)),
                device_id_type=MESH,
            ).start()

    def grad_copy(section):
        first, length = parcels[section]
        whole = pl.ds(first, length)
        return pltpu.make_async_copy(sum_ref.at[whole], grads_out.at[whole], out_sem.at[2 + section])

    def finish(section, k):
        depth, step, group = stage_of(section, k)
        keep, share = spans[section][step + 1]
        moved = pl.ds(landing[section][step if k < depth else 0], (size(group) - 1) * share)
        for sem in (sum_send, sum_recv):
            ref = rbuf if k < depth else sum_ref
            pltpu.make_async_copy(ref.at[moved], ref.at[moved], sem.at[section, k]).wait()
        if k < depth:
            here = pl.ds(keep, share)
            summed = g_ref[here]
            for d in range(1, size(group)):
                landed = rbuf[pl.ds(landing[section][step] + (d - 1) * share, share)]
                summed = summed + landed.astype(f32)
            if k == depth - 1:
                sum_ref[here] = summed.astype(bf16)
            else:
                g_ref[here] = summed
        elif k == 2 * depth - 1:
            grad_copy(section).start()

    def turn(section, k):
        last = 2 * len(orders[section]) - 1
        if 0 <= k <= last:
            finish(section, k)
        if k < last:
            begin(section, k + 1)

    new_copy = pltpu.make_async_copy(new_ref, new_out, out_sem.at[0])
    new_copy.start()

    @pl.loop(0, height // part)
    def _(c):
        back_reset(1, x1, grad_ref, z1, r1, dq1, dzr1, c)

    blocks_h, blocks_v = width // part, height // part
    weight_grads(1, (0, 1), blocks_v, dzr1, plain(x1))
    weight_grads(1, (2,), blocks_v, dq1, lambda first: gated(x1, rx1, (pl.ds(first, part), slice(None))))
    turn(0, -1)

    @pl.loop(0, height // part)
    def _(c):
        rows = pl.ds(pl.multiple_of(c * part, part), part)
        g0[:, rows] = jnp.swapaxes(back_hidden(1, r1, dzr1, c), 0, 1)

    @pl.loop(0, width // part)
    def _(c):
        here = pl.ds(c * part, part)
        inner = pl.ds(c * part + 2, part)
        own = x0[inner, :, pl.ds(0, hd)].astype(f32)
        deltas(g0[here], z0[here], q0[here], own, dq0, dzr0, inner)

    send_edges(dq0, 0)
    turn(0, 0)
    weight_grads(0, (2,), blocks_h, dq0, lambda first: gated(x0, rx0, (pl.ds(first, part), slice(None))))
    weight_grads(0, (0,), blocks_h, dzr0, plain(x0))
    turn(1, -1)
    wait_edges(dq0, 0)

    @pl.loop(0, width // part)
    def _(c):
        back_reset(0, x0, g0, z0, r0, dq0, dzr0, c)

    send_edges(dzr0, 1)
    turn(0, 1)
    turn(1, 0)
    weight_grads(0, (1,), blocks_h, dzr0, plain(x0))
    turn(2, -1)
    wait_edges(dzr0, 1)

    @pl.loop(0, width // part)
    def _(c):
        cols = pl.ds(pl.multiple_of(c * part, part), part)
        hidden_back_ref[:, cols] = jnp.swapaxes(back_hidden(0, r0, dzr0, c), 0, 1)

    back_copy = pltpu.make_async_copy(hidden_back_ref, hidden_back_out, out_sem.at[1])
    back_copy.start()

    for k in range(2 * len(steps)):
        turn(2, k)
        turn(1, k + 1)
        turn(0, k + 2)

    new_copy.wait()
    back_copy.wait()
    for section in range(len(parcels)):
        grad_copy(section).wait()
    pl.when(has_left)(lambda: note.wait_send())
    for c in range(BAND_CHUNKS):
        pl.when((odd == 0) & has_next)(lambda c=c: block_copy(BESIDE, c, True).wait_send())
    for c in range(bands):
        pl.when(has_right)(lambda c=c: score_copy(0, c).wait_send())
        pl.when(has_next)(lambda c=c: score_copy(1, c).wait_send())


def finish_kernel(
    places, new_in, back_in, sums_in, new_out, back_out, grads_out, new, back, sums, rows, grads, sems
):
    sections, gates = 2, len(places) // 2
    taps, mixed = grads.shape[1:3]
    depth = mixed // sections
    piece = -(-depth // 8) * 8
    load = pltpu.make_async_copy(sums_in, sums, sems.at[0])
    load.start()
    enter = [pltpu.make_async_copy(new_in, new, sems.at[1]), pltpu.make_async_copy(back_in, back, sems.at[2])]
    for copy in enter:
        copy.start()
    load.wait()
    through = []
    for gate in range(gates):
        for section in range(sections):
            first = places[section, gate]
            there = pl.ds(first // 16 * 16, -(-(first + taps * piece) // 16) * 16 - first // 16 * 16)
            rows[there] = sums[there].astype(jnp.float32)
            for tap in range(taps):
                taken = rows[pl.ds(first + tap * piece, depth)]
                grads[gate, tap, pl.ds(section, depth, stride=sections)] = taken
        through.append(pltpu.make_async_copy(grads.at[gate], grads_out.at[gate], sems.at[3 + gate]))
        through[-1].start()
        if gate == 0:
            for copy in enter:
                copy.wait()
            for at, (held, out) in enumerate(((new, new_out), (back, back_out))):
                through.append(pltpu.make_async_copy(held, out, sems.at[1 + at]))
                through[-1].start()
    for copy in through:
        copy.wait()


def finished(new_hidden, hidden_back, sums, places, shape):
    anywhere = pl.BlockSpec(memory_space=pl.ANY)
    f32 = jnp.float32
    return pl.pallas_call(
        functools.partial(finish_kernel, places),
        out_shape=(
            jax.ShapeDtypeStruct(new_hidden.shape, new_hidden.dtype),
            jax.ShapeDtypeStruct(hidden_back.shape, hidden_back.dtype),
            jax.ShapeDtypeStruct(shape, f32),
        ),
        in_specs=[anywhere] * 3,
        out_specs=(anywhere,) * 3,
        scratch_shapes=[
            pltpu.VMEM(new_hidden.shape, new_hidden.dtype),
            pltpu.VMEM(hidden_back.shape, hidden_back.dtype),
            pltpu.VMEM(sums.shape, sums.dtype),
            pltpu.VMEM(sums.shape, f32),
            pltpu.VMEM(shape, f32),
            pltpu.SemaphoreType.DMA((3 + shape[0],)),
        ],
        compiler_params=pltpu.CompilerParams(vmem_limit_bytes=58 * 1024 * 1024),
        name="finish",
    )(new_hidden, hidden_back, sums)


def core(offset, block, left, table, hidden, context, weights, hidden_grad, pairs, count, piece):
    height, width, hd = hidden.shape
    taps = weights.shape[1]
    bf16, f32 = jnp.bfloat16, jnp.float32
    anywhere = pl.BlockSpec(memory_space=pl.ANY)
    steps = sum_steps(pairs, count)
    lanes = hd
    gate_rows = taps * piece
    layout = sum_layout(gate_rows, pairs * count)
    sum_rows = sum(length for _, length in layout[1])

    def held(values):
        return pltpu.VMEM(values.shape, values.dtype)

    across = (width, height, hd)
    down = (height, width, hd)

    def padded(shape, wide):
        return pltpu.VMEM((shape[0] + 4, shape[1], wide * hd), bf16)

    return pl.pallas_call(
        functools.partial(core_kernel, count, piece, steps, layout),
        out_shape=(
            jax.ShapeDtypeStruct(hidden.shape, bf16),
            jax.ShapeDtypeStruct(hidden.shape, f32),
            jax.ShapeDtypeStruct((sum_rows, hd), bf16),
        ),
        in_specs=[pl.BlockSpec(memory_space=pltpu.SMEM)] + [anywhere] * 7,
        out_specs=(anywhere,) * 3,
        scratch_shapes=[
            held(hidden),
            pltpu.VMEM(hidden.shape, f32),
            pltpu.VMEM((sum_rows, hd), bf16),
            held(block),
            held(block),
            held(left),
            held(left),
            held(left),
            pltpu.VMEM((5, height // 16, width * width // lanes, 16, lanes), bf16),
            pltpu.VMEM((2, width, lanes), f32),
            held(table),
            held(hidden),
            held(context),
            held(weights),
            pltpu.VMEM((4 * hd, weights.shape[2]), bf16),
            held(hidden_grad),
            pltpu.VMEM((2, 3, taps, 2 * hd, hd), bf16),
            pltpu.VMEM((sum_rows, hd), f32),
            pltpu.VMEM((sum_rows, hd), bf16),
            pltpu.VMEM((sum_rows, hd), bf16),
            padded(across, 2),
            padded(down, 2),
            padded(across, 1),
            padded(down, 1),
            padded(across, 1),
            padded(down, 1),
            padded(across, 2),
            padded(down, 2),
            pltpu.VMEM((3,) + across, f32),
            pltpu.VMEM(across, f32),
            pltpu.VMEM(across, f32),
            pltpu.VMEM(across, f32),
            pltpu.VMEM(down, f32),
            pltpu.VMEM(down, f32),
            pltpu.VMEM(across, f32),
            pltpu.VMEM((taps, 2 * hd, 2 * hd), f32),
            pltpu.SemaphoreType.DMA((2, 2)),
            pltpu.SemaphoreType.DMA((2, 2)),
            pltpu.SemaphoreType.DMA((3, BAND_CHUNKS)),
            pltpu.SemaphoreType.DMA((3, BAND_CHUNKS)),
            pltpu.SemaphoreType.DMA((2, height // 16)),
            pltpu.SemaphoreType.DMA((2, height // 16)),
            pltpu.SemaphoreType.DMA(()),
            pltpu.SemaphoreType.DMA(()),
            pltpu.SemaphoreType.DMA((2, height // 16, 2)),
            pltpu.SemaphoreType.DMA((2, height // 16, 2)),
            pltpu.SemaphoreType.DMA((3, 2 * len(steps))),
            pltpu.SemaphoreType.DMA((3, 2 * len(steps))),
            pltpu.SemaphoreType.DMA((7,)),
            pltpu.SemaphoreType.DMA((5,)),
        ],
        compiler_params=pltpu.CompilerParams(
            collective_id=0, has_side_effects=True, vmem_limit_bytes=58 * 1024 * 1024
        ),
        name="core",
    )(offset, block, left, table, hidden, context, weights, hidden_grad)


def on_device(left_feats, right_feats, offsets, hidden, context, gru_weights, hidden_grad):
    left_block = left_feats[0]
    right_block = right_feats[0]
    column_count = left_block.shape[1]
    table = lookup_table(column_count, LEVELS, RADIUS) / math.sqrt(left_block.shape[-1])
    hd = gru_weights.shape[-1]
    table = packed_table(table, hd)
    table = jnp.asarray(table, jnp.bfloat16)
    pairs, blks = lax.axis_size("pair"), lax.axis_size("blk")
    shape = gru_weights.shape
    piece = -(-shape[3] // 8) * 8
    gate_rows = shape[2] * piece
    mixed = shape[1:3] + (shape[0] * shape[3], hd)
    new_hidden, hidden_back, sums = core(
        offsets,
        right_block,
        left_block,
        table,
        hidden[0],
        context[0],
        jnp.transpose(gru_weights, (1, 2, 3, 0, 4)).reshape(mixed),
        hidden_grad[0],
        pairs,
        blks,
        piece,
    )
    places = sum_layout(gate_rows, pairs * blks)[0]
    new_hidden, hidden_back, grads = finished(new_hidden, hidden_back, sums, places, mixed)
    grads = grads.reshape(shape[1:4] + (shape[0], hd))
    return (new_hidden[None], jnp.transpose(grads, (3, 0, 1, 2, 4)), hidden_back[None])


def solution(mesh):
    placed = (
        P("pair", None, "blk", None),
        P("pair", None, "blk", None),
        P("blk"),
        P("pair", None, "blk", None),
        P("pair", None, None, "blk", None),
        P(),
        P("pair", None, "blk", None),
    )
    return jax.shard_map(
        on_device,
        mesh=mesh,
        in_specs=placed,
        out_specs=(P("pair", None, "blk", None), P(), P("pair", None, "blk", None)),
        check_vma=False,
    )
```
